512 devices in a mesh: ctx: 32 (over y, z_hi), hg: 16 (over z_lo, x, core).
Axes of the slice: x: 4, y: 8, z: 8 (z_hi: 4, z_lo: 2; z = z_hi * 2 + z_lo), core: 2. Of those that a mesh axis runs over, the one named last changes fastest.
Arguments:
- query: bfloat16 [4096, 12288], P('ctx', 'hg'), may hold values from -100 to 100
- latent: bfloat16 [4096, 576], P('ctx'), may hold values from -6 to 6
- w_uk: bfloat16 [512, 8192], P(None, 'hg'), may hold values from -0.25 to 0.25
- w_uv: bfloat16 [512, 8192], P(None, 'hg'), may hold values from -0.25 to 0.25
- w_o: bfloat16 [8192, 7168], P('hg', 'ctx'), may hold values from -0.125 to 0.125
- visible: int32 [64, 64], replicated, may hold values from 0 to 1, as said below
Outputs:
- output: bfloat16 [4096, 7168], P('ctx', 'hg')
The draws below stay inside these ranges and needn't reach their ends.
Inputs may be any that keep to these rules, and one draw needn't show every extreme that they name: visible[q, q] = 1 and visible[q, k] = 0 where k > q.
All inputs are finite; a program needn't handle non-finite values.
Results may differ from the reference program's by a relative error of at most 0.023.
Values may be sent and summed in bfloat16 or wider, within the bound.
A program may use at most 128 MiB of HBM per device.

```python
import math
import jax
import jax.numpy as jnp
from jax import lax

D = 7168
HEADS = 64
NOPE = 128
ROPE = 64
LATENT = 512
VHEAD = 128
TOK_HALF = 64
TOK_DEV = 128
TOKENS = 4096
BLOCKS = 64
N_CTX = 32
N_HG = 16


def latent_values(key):
    draw_seed = jax.random.fold_in(key, 5)
    full_shape = (TOKENS, LATENT + ROPE)
    drawn = jnp.clip(jax.random.normal(draw_seed, full_shape, jnp.float32), -6.0, 6.0)
    return drawn


def draw_latent(key, part):
    return latent_values(key).astype(jnp.bfloat16)


def draw_query(key, part):
    draw_seed = jax.random.fold_in(key, 9)
    full_shape = (TOKENS, HEADS, NOPE + ROPE)
    drawn = jnp.clip(jax.random.normal(draw_seed, full_shape, jnp.float32), -6.0, 6.0)
    return drawn.reshape(TOKENS, HEADS * (NOPE + ROPE)).astype(jnp.bfloat16)


def draw_visible(key, part):
    random_bits = jax.random.randint(jax.random.fold_in(key, 3), (BLOCKS, BLOCKS), 0, 2)
    block_ids = jnp.arange(BLOCKS)
    below_diagonal = block_ids[:, None] > block_ids[None, :]
    on_diagonal = block_ids[:, None] == block_ids[None, :]
    return jnp.where(on_diagonal, 1, jnp.where(below_diagonal, random_bits, 0)).astype(jnp.int32)


def raised(values, key, source, target, shards_of, factor):
    def block_of(position):
        return (jnp.arange(values.shape[position]) // (values.shape[position] // shards_of)).reshape((-1,) + (1,) * (values.ndim - 1 - position))

    one_side = jax.random.permutation(key, shards_of)[block_of(target)]
    far = (block_of(target) + shards_of // 2) % shards_of
    return jnp.where((block_of(source) == one_side) | (block_of(source) == far), factor * values, values)


def block_scale(own_key, shape, split, least, top_value):
    level = 1.0
    for position, shards_of in split:
        steps = jax.random.uniform(jax.random.fold_in(jax.random.fold_in(own_key, 6), position), (shards_of,), jnp.float32, least / len(split), top_value / len(split))
        level = level * jnp.repeat(jnp.exp(steps), shape[position] // shards_of).reshape((-1,) + (1,) * (len(shape) - 1 - position))
    return level


def noise(key, dims, spread, reach, pieces=(), held_as=jnp.bfloat16):
    values = jax.random.normal(key, dims, jnp.float32) * spread
    if len(pieces) > 0:
        values = block_scale(key, dims, pieces, -0.22, 0.18) * values
    return jnp.clip(values, min=-reach, max=reach).astype(held_as)


def gaussian_with(key, shape, deviation, most, cuts, heavy, held_as=jnp.bfloat16):
    values = deviation * jax.random.normal(key, shape, jnp.float32)
    if cuts:
        values = values * block_scale(key, shape, cuts, -0.22, 0.18)
    return jnp.clip(raised(values, jax.random.fold_in(key, 3), *heavy), -most, most).astype(held_as)


def setup_inputs(seed: int = 0) -> dict:
    arg_keys = jax.random.split(jax.random.key(seed), 7)
    query = draw_query(jax.random.fold_in(arg_keys[6], 71), 0)
    latent = draw_latent(jax.random.fold_in(arg_keys[6], 71), 0)
    w_uk = noise(arg_keys[2], (LATENT, HEADS * NOPE), LATENT ** -0.5, 0.25, ((1, 16),))
    w_uv = noise(arg_keys[3], (LATENT, HEADS * VHEAD), LATENT ** -0.5, 0.25, ((1, 16),))
    w_o = gaussian_with(arg_keys[4], (HEADS * VHEAD, D), (HEADS * VHEAD) ** -0.5, 0.125, ((0, 16), (1, 32)), (0, 1, 32, 2.75))
    visible = draw_visible(jax.random.fold_in(arg_keys[6], 71), 0)
    return {"query": query, "latent": latent, "w_uk": w_uk, "w_uv": w_uv, "w_o": w_o, "visible": visible}


def seq_blocks(row_ids):
    source = row_ids // TOK_DEV
    within = row_ids % TOK_DEV
    return jnp.where(within < TOK_HALF, source, 2 * N_CTX - 1 - source).astype(jnp.int32)

def reference(query, latent, w_uk, w_uv, w_o, visible):
    row_ids = jnp.arange(TOKENS, dtype=jnp.int32)
    block_of = seq_blocks(row_ids)
    positions = block_of * TOK_HALF + row_ids % TOK_DEV % TOK_HALF
    allowed = (visible[block_of][:, block_of] == 1) & (positions[None, :] <= positions[:, None])
    compact = latent[:, :LATENT].astype(jnp.float32)
    key_rotary = latent[:, LATENT:].astype(jnp.float32)
    expanded_keys = jnp.dot(compact, w_uk.astype(jnp.float32)).astype(jnp.bfloat16)
    expanded_values = jnp.dot(compact, w_uv.astype(jnp.float32)).astype(jnp.bfloat16)
    expanded_keys = lax.optimization_barrier(expanded_keys)
    expanded_values = lax.optimization_barrier(expanded_values)
    queries = query.astype(jnp.float32).reshape(TOKENS, HEADS, NOPE + ROPE).transpose(1, 0, 2)
    keys_heads = expanded_keys.astype(jnp.float32).reshape(TOKENS, HEADS, NOPE).transpose(1, 0, 2)
    values_heads = expanded_values.astype(jnp.float32).reshape(TOKENS, HEADS, VHEAD).transpose(1, 0, 2)
    score_scale = 1.0 / math.sqrt(NOPE + ROPE)

    def one_head(operands):
        query_head, key_head, value_head = operands
        scores = (jnp.dot(query_head[:, :NOPE], key_head.T) + jnp.dot(query_head[:, NOPE:], key_rotary.T)) * score_scale
        masked = jnp.where(allowed, scores, -jnp.inf)
        row_max = lax.optimization_barrier(jnp.max(masked, axis=1, keepdims=True))
        weights = jnp.where(allowed, jnp.exp(masked - row_max), jnp.float32(0.0))
        row_total = lax.optimization_barrier(jnp.sum(weights, axis=1, keepdims=True))
        rounded = lax.optimization_barrier(weights.astype(jnp.bfloat16)).astype(jnp.float32)
        blended = jnp.dot(rounded, value_head) / row_total
        return blended.astype(jnp.bfloat16)
    heads_out = lax.map(one_head, (queries, keys_heads, values_heads))
    attended = heads_out.transpose(1, 0, 2).reshape(TOKENS, HEADS * VHEAD)
    group_width = HEADS * VHEAD // N_HG
    summed = jnp.zeros((TOKENS, D), jnp.float32)
    for group_number in range(N_HG):
        lower_edge = group_number * group_width
        partial_term = jnp.dot(attended[:, lower_edge:lower_edge + group_width].astype(jnp.float32), w_o[lower_edge:lower_edge + group_width].astype(jnp.float32))
        partial_term = lax.optimization_barrier(partial_term.astype(jnp.bfloat16))
        summed = summed + partial_term.astype(jnp.float32)
    return summed.astype(jnp.bfloat16)
```

```python
import functools
import math

import jax
import jax.numpy as jnp
from jax import lax
from jax.experimental import pallas as pl
from jax.experimental.pallas import tpu as pltpu
from jax.sharding import PartitionSpec as P

NOPE = 128
ROPE = 64
LATENT = 512
VHEAD = 128
NY, NZH, NZL, NX, NCORE = 8, 4, 2, 4, 2
NCTX = NY * NZH
NCHIP = NZL * NX
MESH = pl.DeviceIdType.MESH


def place():
    c = lax.axis_index("ctx")
    h = lax.axis_index("hg")
    y, k = c // NZH, c % NZH
    chip, core = h // NCORE, h % NCORE
    zl, x = chip // NX, chip % NX
    return y, k, zl, x, core


def device(y, k, zl, x, core):
    return (
        lax.rem(y + NY, NY) * NZH + lax.rem(k + NZH, NZH),
        (zl * NX + lax.rem(x + NX, NX)) * NCORE + core,
    )


def remote(src, dst, send, recv, dev):
    return pltpu.make_async_remote_copy(
        src_ref=src, dst_ref=dst, send_sem=send, recv_sem=recv, device_id=dev, device_id_type=MESH
    )


def greet(devices):
    barrier = pltpu.get_barrier_semaphore()
    for dev in devices:
        pl.semaphore_signal(barrier, inc=1, device_id=dev, device_id_type=MESH)
    return barrier


def gather_kernel(
    lat_ref,
    wo_ref,
    all_ref,
    wog_ref,
    own_sem,
    z_send,
    z_recv,
    r_send,
    r_recv,
    l_send,
    l_recv,
    x_send,
    x_recv,
    sib_send,
    sib_recv,
    wo_send,
    wo_recv,
):
    y, k, zl, x, core = place()
    rows = lat_ref.shape[0]
    half = rows // 2
    quarter = half // NX
    d = 2 * zl - 1
    me = y * NZH + k
    sibling = device(y, k, zl, x, 1 - core)
    line = [device(y, k + j, zl, x, core) for j in (1, 2, 3)]
    line += [device(y, k + j, zl, x, 1 - core) for j in range(NZH)]
    z_targets = [
        device(y, k + d, zl, x, core),
        device(y, k + d, 1 - zl, x, core),
        device(y, k + 2, 1 - zl, x, core),
    ]
    up, down = device(y + 1, k, zl, x, core), device(y - 1, k, zl, x, core)
    x_peers = [device(y, k, zl, x + j, core) for j in (1, 2, 3)]
    partners = line + z_targets[1:] + [up, down] + x_peers
    barrier = greet(partners)
    pl.semaphore_wait(barrier, len(partners))

    def blk(yy, kk):
        return lax.rem(yy + NY, NY) * NZH + lax.rem(kk + NZH, NZH)

    own = pltpu.make_async_copy(lat_ref, all_ref.at[me], own_sem)
    own.start()
    base = pl.multiple_of(core * half, half)
    part = pl.ds(base, half)
    z_copies = []
    for j, target in enumerate(z_targets):
        copy = remote(
            lat_ref.at[part, :], all_ref.at[me, part, :], z_send.at[j], z_recv.at[j], target
        )
        copy.start()
        z_copies.append(copy)
    order = [k, k - d, k + d, k + 2]

    def z_wait(j):
        src = all_ref.at[blk(y, order[j + 1]), part, :]
        remote(src, src, z_send.at[j], z_recv.at[j], z_targets[j]).wait_recv()

    def ring(row0, nrows, forward):
        span = pl.ds(row0, nrows)

        def up_copy(step, j, wait):
            yy = y - step if wait else y - step + 1
            ref = all_ref.at[blk(yy, order[j]), span, :]
            return remote(ref, ref, r_send.at[step - 1, j], r_recv.at[step - 1, j], up)

        def down_copy(step, j, wait):
            yy = y + step if wait else y + step - 1
            ref = all_ref.at[blk(yy, order[j]), span, :]
            return remote(ref, ref, l_send.at[step - 1, j], l_recv.at[step - 1, j], down)

        def goes_up(step, j):
            return step < 4 or (step == 4 and j < 2)

        def goes_down(step, j):
            return step < 4 or (step == 4 and j >= 2)

        own.wait()
        for j in range(NZH):
            if j > 0:
                z_wait(j - 1)
                ref = all_ref.at[blk(y, order[j]), part, :]
                remote(ref, ref, sib_send.at[j], sib_recv.at[j], sibling).start()
            up_copy(1, j, False).start()
            down_copy(1, j, False).start()
        for step in (1, 2, 3, 4):
            for j in range(NZH):
                if goes_up(step, j):
                    up_copy(step, j, True).wait_recv()
                    if goes_up(step + 1, j):
                        up_copy(step + 1, j, False).start()
                if goes_down(step, j):
                    down_copy(step, j, True).wait_recv()
                    if goes_down(step + 1, j):
                        down_copy(step + 1, j, False).start()
            forward(2 * step - 2, y - step)
            if step < 4:
                forward(2 * step - 1, y + step)
        for step in (1, 2, 3, 4):
            for j in range(NZH):
                if goes_up(step, j):
                    up_copy(step, j, False).wait_send()
                if goes_down(step, j):
                    down_copy(step, j, False).wait_send()

    def group(yy, row0, nrows):
        return all_ref.at[pl.ds(blk(yy, 0), NZH), pl.ds(row0, nrows), :]

    def visits():
        for step in (1, 2, 3, 4):
            yield 2 * step - 2, y - step
            if step < 4:
                yield 2 * step - 1, y + step

    def wo_copies():
        for j in (1, 2, 3):
            yield j, remote(
                wo_ref,
                wog_ref.at[k % 2, core],
                wo_send.at[j],
                wo_recv.at[k % 2, core],
                device(y, k + j, zl, x, k // 2),
            )

    wo_here = core == k // 2
    wo_stay = pltpu.make_async_copy(wo_ref, wog_ref.at[k % 2, core], wo_send.at[0])
    wo_pass = remote(
        wo_ref, wog_ref.at[k % 2, core], wo_send.at[0], wo_recv.at[k % 2, core], sibling
    )
    for _, copy in wo_copies():
        copy.start()

    @pl.when(wo_here)
    def _():
        wo_stay.start()

    @pl.when(jnp.logical_not(wo_here))
    def _():
        wo_pass.start()

    def sib_slot(n, q):
        return 4 + n * NX + q

    @pl.when(core == 0)
    def _():
        def forward(n, yy):
            ref = group(yy, 0, half)
            remote(ref, ref, sib_send.at[sib_slot(n, 0)], sib_recv.at[sib_slot(n, 0)], sibling).start()

        ring(0, half, forward)
        for n, yy in visits():
            ref = group(yy, 0, half)
            remote(ref, ref, sib_send.at[sib_slot(n, 0)], sib_recv.at[sib_slot(n, 0)], sibling).wait_send()
        for j in (1, 2, 3):
            ref = all_ref.at[blk(y, order[j]), pl.ds(half, half), :]
            remote(ref, ref, sib_send.at[j], sib_recv.at[j], sibling).wait_recv()
        for n, yy in visits():
            for q in range(NX):
                ref = group(yy, pl.multiple_of(half + lax.rem(x + q, NX) * quarter, quarter), quarter)
                remote(
                    ref, ref, sib_send.at[sib_slot(n, q)], sib_recv.at[sib_slot(n, q)], sibling
                ).wait_recv()

    @pl.when(core == 1)
    def _():
        mine = pl.multiple_of(half + x * quarter, quarter)

        def x_copy(n, yy, q):
            ref = group(yy, mine, quarter)
            return remote(ref, ref, x_send.at[n, q], x_recv.at[n, q], x_peers[q - 1])

        def to_sibling(n, yy, q):
            ref = group(yy, pl.multiple_of(half + lax.rem(x + q, NX) * quarter, quarter), quarter)
            return remote(
                ref, ref, sib_send.at[sib_slot(n, q)], sib_recv.at[sib_slot(n, q)], sibling
            )

        def forward(n, yy):
            for q in (1, 2, 3):
                x_copy(n, yy, q).start()
            to_sibling(n, yy, 0).start()

        ring(mine, quarter, forward)
        for n, yy in visits():
            for q in (1, 2, 3):
                ref = group(yy, pl.multiple_of(half + lax.rem(x + q, NX) * quarter, quarter), quarter)
                remote(ref, ref, x_send.at[n, NX - q], x_recv.at[n, NX - q], x_peers[q - 1]).wait_recv()
                to_sibling(n, yy, q).start()
        for n, yy in visits():
            for q in (1, 2, 3):
                x_copy(n, yy, q).wait_send()
            for q in range(NX):
                to_sibling(n, yy, q).wait_send()
        for j in (1, 2, 3):
            ref = all_ref.at[blk(y, order[j]), pl.ds(0, half), :]
            remote(ref, ref, sib_send.at[j], sib_recv.at[j], sibling).wait_recv()
        for n, yy in visits():
            ref = group(yy, 0, half)
            remote(ref, ref, sib_send.at[sib_slot(n, 0)], sib_recv.at[sib_slot(n, 0)], sibling).wait_recv()

    for j in (1, 2, 3):
        ref = all_ref.at[blk(y, order[j]), part, :]
        remote(ref, ref, sib_send.at[j], sib_recv.at[j], sibling).wait_send()
    for copy in z_copies:
        copy.wait_send()
    for _, copy in wo_copies():
        copy.wait_send()

    @pl.when(wo_here)
    def _():
        wo_stay.wait()

    @pl.when(jnp.logical_not(wo_here))
    def _():
        wo_pass.wait_send()

    for r in range(2):
        for s in range(2):
            @pl.when(jnp.logical_not((k == 2 * core + r) & (core == s)))
            def _():
                ref = wog_ref.at[r, s]
                remote(ref, ref, wo_send.at[0], wo_recv.at[r, s], sibling).wait_recv()


def gather(latent, w_o):
    rows, width = latent.shape
    inner, cols = w_o.shape
    dma = pltpu.SemaphoreType.DMA
    return pl.pallas_call(
        gather_kernel,
        out_shape=(
            jax.ShapeDtypeStruct((NCTX, rows, width), latent.dtype),
            jax.ShapeDtypeStruct((2, NCORE, inner, cols), w_o.dtype),
        ),
        in_specs=[pl.BlockSpec(memory_space=pltpu.VMEM)] * 2,
        out_specs=(pl.BlockSpec(memory_space=pltpu.VMEM),) * 2,
        scratch_shapes=[
            dma,
            dma((3,)),
            dma((3,)),
            dma((4, NZH)),
            dma((4, NZH)),
            dma((4, NZH)),
            dma((4, NZH)),
            dma((7, NX)),
            dma((7, NX)),
            dma((4 + 7 * NX,)),
            dma((4 + 7 * NX,)),
            dma((4,)),
            dma((2, NCORE)),
        ],
        compiler_params=pltpu.CompilerParams(
            collective_id=0, has_side_effects=True, vmem_limit_bytes=40 << 20
        ),
        name="gather_latent",
    )(latent, w_o)


def project_kernel(
    att_ref,
    wo_ref,
    out_ref,
    blocks,
    outgoing,
    incoming,
    kept,
    final,
    r_send,
    r_recv,
    l_send,
    l_recv,
    sib_send,
    sib_recv,
    p_send,
    p_recv,
    f_send,
    f_recv,
):
    y, k, zl, x, core = place()
    chip = zl * NX + x
    rows, inner = att_ref.shape
    sibling = device(y, k, zl, x, 1 - core)
    up, down = device(y + 1, k, zl, x, core), device(y - 1, k, zl, x, core)
    peers = [
        (y * NZH + k, lax.rem(chip + j, NCHIP) * NCORE + core) for j in range(1, NCHIP)
    ]
    last = (chip * NZH + k, y * NCORE + core)
    moves = chip != y
    partners = [sibling, up, down] + peers
    barrier = greet(partners)

    @pl.when(moves)
    def _():
        pl.semaphore_signal(barrier, inc=1, device_id=last, device_id_type=MESH)

    pl.semaphore_wait(barrier, len(partners) + jnp.where(moves, 1, 0))

    def at(yy):
        return lax.rem(yy + NY, NY)

    top, bottom = pl.ds(0, rows // 2), pl.ds(rows // 2, rows // 2)

    def span(step, going_up):
        if step < 4:
            return pl.ds(0, rows)
        return top if going_up else bottom

    def up_copy(step, wait):
        yy = at(y - step) if wait else at(y - step + 1)
        ref = blocks.at[core, yy, span(step, True), :]
        return remote(ref, ref, r_send.at[step - 1], r_recv.at[step - 1], up)

    def down_copy(step, wait):
        yy = at(y + step) if wait else at(y + step - 1)
        ref = blocks.at[core, yy, span(step, False), :]
        return remote(ref, ref, l_send.at[step - 1], l_recv.at[step - 1], down)

    def sib_copy(n, yy, wait):
        ref = blocks.at[1 - core if wait else core, at(yy)]
        return remote(ref, ref, sib_send.at[n], sib_recv.at[n], sibling)

    def piece_copy(yy):
        return remote(
            outgoing.at[yy],
            incoming.at[chip],
            p_send.at[yy],
            p_recv.at[chip],
            (y * NZH + k, yy * NCORE + core),
        )

    def piece(n, yy):
        sib_copy(n, yy, True).wait_recv()
        yy = at(yy)
        acc = jnp.dot(blocks[0, yy], wo_ref[:inner, :], preferred_element_type=jnp.float32)
        acc += jnp.dot(blocks[1, yy], wo_ref[inner:, :], preferred_element_type=jnp.float32)

        @pl.when(yy == chip)
        def _():
            kept[...] = acc

        @pl.when(yy != chip)
        def _():
            outgoing[yy] = acc.astype(outgoing.dtype)
            piece_copy(yy).start()

    blocks[core, y] = att_ref[...]
    up_copy(1, False).start()
    down_copy(1, False).start()
    sib_copy(0, y, False).start()
    piece(0, y)
    for step in (1, 2, 3):
        up_copy(step, True).wait_recv()
        up_copy(step + 1, False).start()
        sib_copy(2 * step - 1, y - step, False).start()
        down_copy(step, True).wait_recv()
        down_copy(step + 1, False).start()
        sib_copy(2 * step, y + step, False).start()
        piece(2 * step - 1, y - step)
        piece(2 * step, y + step)
    up_copy(4, True).wait_recv()
    down_copy(4, True).wait_recv()
    sib_copy(7, y + 4, False).start()
    piece(7, y + 4)

    total = kept[...]
    for j in range(1, NCHIP):
        source = lax.rem(chip + j, NCHIP)
        ref = incoming.at[source]
        remote(ref, ref, p_send.at[0], p_recv.at[source], peers[j - 1]).wait_recv()
        total += incoming[source].astype(jnp.float32)

    @pl.when(jnp.logical_not(moves))
    def _():
        out_ref[...] = total.astype(out_ref.dtype)

    @pl.when(moves)
    def _():
        final[...] = total.astype(final.dtype)
        copy = remote(final, out_ref, f_send, f_recv, last)
        copy.start()
        copy.wait()

    for step in (1, 2, 3, 4):
        up_copy(step, False).wait_send()
        down_copy(step, False).wait_send()
    visit = [0, -1, 1, -2, 2, -3, 3, 4]
    for n, off in enumerate(visit):
        sib_copy(n, y + off, False).wait_send()
    for j in range(1, NCHIP):
        piece_copy(lax.rem(chip + j, NCHIP)).wait_send()


def project(attended, w_o):
    rows, inner = attended.shape
    cols = w_o.shape[1]
    dma = pltpu.SemaphoreType.DMA
    return pl.pallas_call(
        project_kernel,
        out_shape=jax.ShapeDtypeStruct((rows, cols), attended.dtype),
        in_specs=[pl.BlockSpec(memory_space=pltpu.VMEM)] * 2,
        out_specs=pl.BlockSpec(memory_space=pltpu.VMEM),
        scratch_shapes=[
            pltpu.VMEM((NCORE, NY, rows, inner), attended.dtype),
            pltpu.VMEM((NCHIP, rows, cols), attended.dtype),
            pltpu.VMEM((NCHIP, rows, cols), attended.dtype),
            pltpu.VMEM((rows, cols), jnp.float32),
            pltpu.VMEM((rows, cols), attended.dtype),
            dma((4,)),
            dma((4,)),
            dma((4,)),
            dma((4,)),
            dma((NY,)),
            dma((NY,)),
            dma((NCHIP,)),
            dma((NCHIP,)),
            dma,
            dma,
        ],
        compiler_params=pltpu.CompilerParams(
            collective_id=1, has_side_effects=True, vmem_limit_bytes=40 << 20
        ),
        name="project",
    )(attended, w_o)


def on_device(query, latent, w_uk, w_uv, w_o, visible):
    cycle_size = lax.axis_size("ctx")
    span_index = lax.axis_index("ctx")
    row_count = query.shape[0]
    half_rows = row_count // 2
    group_heads = w_uk.shape[1] // NOPE
    block_count = visible.shape[0]
    block_ids = jnp.arange(block_count, dtype=jnp.int32)

    def seq_block(row_ids):
        source = row_ids // row_count
        within = row_ids % row_count
        return jnp.where(within < half_rows, source, 2 * cycle_size - 1 - source)

    def seq_position(row_ids, block_of):
        return block_of * half_rows + row_ids % row_count % half_rows

    own_rows = span_index * row_count + jnp.arange(row_count, dtype=jnp.int32)
    query_block = seq_block(own_rows)
    query_position = seq_position(own_rows, query_block)
    query_onehot = (query_block[:, None] == block_ids[None, :]).astype(jnp.float32)
    query_visible = jnp.dot(query_onehot, visible.astype(jnp.float32))
    shaped = query.reshape(row_count, group_heads, NOPE + ROPE)
    query_plain = shaped[:, :, :NOPE]
    query_rotary = shaped[:, :, NOPE:]
    score_scale = 1.0 / math.sqrt(NOPE + ROPE)
    blocks, wo_blocks = gather(latent, w_o)
    segment = blocks.reshape(cycle_size * row_count, latent.shape[1])
    wo_cols = wo_blocks.transpose(1, 2, 0, 3).reshape(NCORE * w_o.shape[0], 2 * w_o.shape[1])
    row_ids = jnp.arange(segment.shape[0], dtype=jnp.int32)
    key_block = seq_block(row_ids)
    key_position = seq_position(row_ids, key_block)
    key_onehot = (key_block[:, None] == block_ids[None, :]).astype(jnp.float32)
    seen = jnp.dot(query_visible, key_onehot.T) > 0.5
    allowed = seen & (key_position[None, :] <= query_position[:, None])
    compact = segment[:, :LATENT]
    key_flat = jnp.dot(compact, w_uk, preferred_element_type=jnp.float32).astype(jnp.bfloat16)
    value_flat = jnp.dot(compact, w_uv, preferred_element_type=jnp.float32).astype(jnp.bfloat16)
    seg_rows = key_flat.shape[0]
    expanded_keys = key_flat.reshape(seg_rows, group_heads, NOPE)
    expanded_values = value_flat.reshape(seg_rows, group_heads, VHEAD)
    scores = jnp.einsum(
        "thd,khd->htk", query_plain, expanded_keys, preferred_element_type=jnp.float32
    )
    scores = scores + jnp.einsum(
        "thr,kr->htk", query_rotary, segment[:, LATENT:], preferred_element_type=jnp.float32
    )
    scores = scores * score_scale
    masked = jnp.where(allowed[None], scores, jnp.float32(-1e30))
    row_max = jnp.max(masked, axis=2)
    weights = jnp.where(allowed[None], jnp.exp(masked - row_max[:, :, None]), jnp.float32(0.0))
    row_total = jnp.sum(weights, axis=2)
    accumulated = jnp.einsum(
        "htk,khd->htd",
        weights.astype(jnp.bfloat16),
        expanded_values,
        preferred_element_type=jnp.float32,
    )
    attended = (
        (accumulated / row_total[:, :, None])
        .transpose(1, 0, 2)
        .reshape(row_count, group_heads * VHEAD)
        .astype(jnp.bfloat16)
    )
    return project(attended, wo_cols)


def solution(mesh):
    in_specs = (P("ctx", "hg"), P("ctx", None), P(None, "hg"), P(None, "hg"), P("hg", "ctx"), P())
    out_specs = P("ctx", "hg")
    return jax.shard_map(
        on_device, mesh=mesh, in_specs=in_specs, out_specs=out_specs, check_vma=False
    )
```

```python
import math

import jax
import jax.numpy as jnp
from jax import lax
from jax.experimental import pallas as pl
from jax.experimental.pallas import tpu as pltpu
from jax.sharding import PartitionSpec as P

NOPE = 128
ROPE = 64
LATENT = 512
VHEAD = 128
NY, NZH, NZL, NX, NCORE = 8, 4, 2, 4, 2
NCTX = NY * NZH
NCHIP = NZL * NX
MESH = pl.DeviceIdType.MESH
MASKED = -1e30
BF16 = jnp.bfloat16
F32 = jnp.float32


def place():
    c = lax.axis_index("ctx")
    h = lax.axis_index("hg")
    y, k = c // NZH, c % NZH
    chip, core = h // NCORE, h % NCORE
    zl, x = chip // NX, chip % NX
    return y, k, zl, x, core


def device(y, k, zl, x, core):
    return (
        lax.rem(y + NY, NY) * NZH + lax.rem(k + NZH, NZH),
        (zl * NX + lax.rem(x + NX, NX)) * NCORE + core,
    )


def block_of(y, k):
    return lax.rem(y + NY, NY) * NZH + lax.rem(k + NZH, NZH)


def remote(src, dst, send, recv, dev):
    return pltpu.make_async_remote_copy(
        src_ref=src, dst_ref=dst, send_sem=send, recv_sem=recv, device_id=dev, device_id_type=MESH
    )


def nt_dot(a, b):
    return lax.dot_general(a, b, (((1,), (1,)), ((), ())), preferred_element_type=F32)


def layer_kernel(
    q_hbm,
    lat_hbm,
    wk_hbm,
    wv_hbm,
    wo_hbm,
    vis_hbm,
    out_ref,
    q_ref,
    lat_ref,
    wk_ref,
    wv_ref,
    wo_ref,
    vis_ref,
    all_ref,
    wog_ref,
    wkt,
    wvt,
    qaug,
    diag,
    m_ref,
    l_ref,
    acc_ref,
    blocks,
    outgoing,
    incoming,
    kept,
    final,
    in_sem,
    z_send,
    z_recv,
    r_send,
    r_recv,
    l_send,
    l_recv,
    x_send,
    x_recv,
    sib_send,
    sib_recv,
    wo_send,
    wo_recv,
    ar_send,
    ar_recv,
    al_send,
    al_recv,
    as_send,
    as_recv,
    p_send,
    p_recv,
    f_send,
    f_recv,
):
    y, k, zl, x, core = place()
    chip = zl * NX + x
    width, rows = lat_ref.shape
    heads = wkt.shape[0]
    half = width // 2
    quarter = half // NX
    d = 2 * zl - 1
    me = y * NZH + k
    sibling = device(y, k, zl, x, 1 - core)
    line = [device(y, k + j, zl, x, core) for j in (1, 2, 3)]
    line += [device(y, k + j, zl, x, 1 - core) for j in range(NZH)]
    z_targets = [
        device(y, k + d, 1 - zl, x, core),
        device(y, k + d, zl, x, core),
        device(y, k + 2, 1 - zl, x, core),
    ]
    up, down = device(y + 1, k, zl, x, core), device(y - 1, k, zl, x, core)
    x_peers = [device(y, k, zl, x + j, core) for j in (1, 2, 3)]
    chips = [(me, lax.rem(chip + j, NCHIP) * NCORE + core) for j in range(1, NCHIP)]
    last = (chip * NZH + k, y * NCORE + core)
    moves = chip != y

    loads = [
        pltpu.make_async_copy(src, dst, in_sem.at[i])
        for i, (src, dst) in enumerate(
            (
                (lat_hbm, lat_ref),
                (q_hbm, q_ref),
                (vis_hbm, vis_ref),
                (wk_hbm, wk_ref),
                (wv_hbm, wv_ref),
                (wo_hbm, wo_ref),
            )
        )
    ]
    for load in loads:
        load.start()

    partners = line + [z_targets[0], z_targets[2], up, down] + chips
    barrier = pltpu.get_barrier_semaphore()
    for dev in partners:
        pl.semaphore_signal(barrier, inc=1, device_id=dev, device_id_type=MESH)

    @pl.when(moves)
    def _():
        pl.semaphore_signal(barrier, inc=1, device_id=last, device_id_type=MESH)

    pl.semaphore_wait(barrier, len(partners) + jnp.where(moves, 1, 0))

    loads[0].wait()
    base = pl.multiple_of(core * half, 8)
    part = pl.ds(base, half)
    order = [k, k + d, k - d, k + 2]
    mine = pl.multiple_of(half + x * quarter, 8)

    def z_copy(j):
        return remote(
            lat_ref.at[part, :], all_ref.at[me, part, :], z_send.at[j - 1], z_recv.at[j - 1], z_targets[j - 1]
        )

    for j in (1, 2, 3):
        z_copy(j).start()
    all_ref[me] = lat_ref[...]

    def z_wait(j):
        ref = all_ref.at[block_of(y, order[j]), part, :]
        remote(ref, ref, z_send.at[j - 1], z_recv.at[j - 1], z_targets[j - 1]).wait_recv()

    def z_sib(j, here):
        ref = all_ref.at[block_of(y, order[j]), pl.ds(base if here else half - base, half), :]
        return remote(ref, ref, sib_send.at[j], sib_recv.at[j], sibling)

    def ring_copy(going_up, step, j, row0, count, wait):
        off = step if wait else step - 1
        yy = y - off if going_up else y + off
        ref = all_ref.at[block_of(yy, order[j]), pl.ds(row0, count), :]
        send, recv, dev = (r_send, r_recv, up) if going_up else (l_send, l_recv, down)
        return remote(ref, ref, send.at[step - 1, j], recv.at[step - 1, j], dev)

    def goes(going_up, step, j):
        return step < 4 or (step == 4 and (j < 2) == going_up)

    def ring_step(step, row0, count):
        for j in range(NZH):
            for going_up in (True, False):
                if goes(going_up, step, j):
                    ring_copy(going_up, step, j, row0, count, True).wait_recv()
                    if goes(going_up, step + 1, j):
                        ring_copy(going_up, step + 1, j, row0, count, False).start()

    def groups(step):
        if step == 4:
            return [(6, y - 4)]
        return [(2 * step - 2, y - step), (2 * step - 1, y + step)]

    def group(yy, row0, count):
        return all_ref.at[pl.ds(block_of(yy, 0), NZH), pl.ds(row0, count), :]

    def low_copy(n, yy):
        ref = group(yy, 0, half)
        return remote(ref, ref, sib_send.at[4 + n * NX], sib_recv.at[4 + n * NX], sibling)

    def high_copy(n, yy, q):
        ref = group(yy, pl.multiple_of(half + lax.rem(x + q, NX) * quarter, 8), quarter)
        slot = 4 + n * NX + q
        return remote(ref, ref, sib_send.at[slot], sib_recv.at[slot], sibling)

    def x_copy(n, yy, q):
        ref = group(yy, mine, quarter)
        return remote(ref, ref, x_send.at[n, q], x_recv.at[n, q], x_peers[q - 1])

    def x_wait(n, yy, q):
        ref = group(yy, pl.multiple_of(half + lax.rem(x + q, NX) * quarter, 8), quarter)
        remote(ref, ref, x_send.at[n, NX - q], x_recv.at[n, NX - q], x_peers[q - 1]).wait_recv()

    def ring_start(j):
        @pl.when(core == 0)
        def _():
            ring_copy(True, 1, j, 0, half, False).start()
            ring_copy(False, 1, j, 0, half, False).start()

        @pl.when(core == 1)
        def _():
            ring_copy(True, 1, j, mine, quarter, False).start()
            ring_copy(False, 1, j, mine, quarter, False).start()

    ring_start(0)

    wo_slot = wog_ref.at[k % 2, core]
    wo_here = core == k // 2
    wo_stay = pltpu.make_async_copy(wo_ref, wo_slot, wo_send.at[0])
    wo_pass = remote(wo_ref, wo_slot, wo_send.at[0], wo_recv.at[k % 2, core], sibling)
    wo_far = [
        remote(wo_ref, wo_slot, wo_send.at[j], wo_recv.at[k % 2, core], device(y, k + j, zl, x, k // 2))
        for j in (1, 2, 3)
    ]

    def first_duties():
        for load in loads[1:]:
            load.wait()
        wkt[...] = wk_ref[...].astype(F32).T.astype(BF16).reshape(wkt.shape)
        wvt[...] = wv_ref[...].astype(F32).T.astype(BF16).reshape(wvt.shape)
        seen = [vis_ref[pl.ds(me, 1), :], vis_ref[pl.ds(2 * NCTX - 1 - me, 1), :]]
        hidden = jnp.concatenate(
            [jnp.broadcast_to(jnp.where(row == 1, 0.0, 1.0), (rows // 2, row.shape[1])) for row in seen], axis=0
        ).astype(BF16)
        for h in range(heads):
            lo = h * (NOPE + ROPE)
            qaug[h] = jnp.concatenate([q_ref[:, lo : lo + NOPE + ROPE], hidden], axis=1)
        i = lax.broadcasted_iota(jnp.int32, diag.shape, 0)
        j = lax.broadcasted_iota(jnp.int32, diag.shape, 1)
        jj = j % rows
        same = (j // rows == k) & (i // (rows // 2) == jj // (rows // 2))
        diag[...] = jnp.where(same & (jj > i), MASKED, 0.0)
        m_ref[...] = jnp.full(m_ref.shape, MASKED, F32)
        l_ref[...] = jnp.zeros(l_ref.shape, F32)
        acc_ref[...] = jnp.zeros(acc_ref.shape, F32)
        for j in (1, 2, 3):
            z_wait(j)
            z_sib(j, True).start()
            ring_start(j)
        for copy in wo_far:
            copy.start()

        @pl.when(wo_here)
        def _():
            wo_stay.start()

        @pl.when(jnp.logical_not(wo_here))
        def _():
            wo_pass.start()

        for j in (1, 2, 3):
            z_sib(j, False).wait_recv()

    def duties(stage):
        if stage <= 4:
            @pl.when(core == 0)
            def _():
                ring_step(stage, 0, half)
                for n, yy in groups(stage):
                    low_copy(n, yy).start()

            @pl.when(core == 1)
            def _():
                ring_step(stage, mine, quarter)
                for n, yy in groups(stage):
                    for q in (1, 2, 3):
                        x_copy(n, yy, q).start()
                    high_copy(n, yy, 0).start()

        if stage == 1:
            diag[...] = jnp.zeros(diag.shape, F32)
        else:
            @pl.when(core == 1)
            def _():
                for n, yy in groups(stage - 1):
                    for q in (1, 2, 3):
                        x_wait(n, yy, q)
                        high_copy(n, yy, q).start()
                for n, yy in groups(stage - 1):
                    low_copy(n, yy).wait_recv()

            @pl.when(core == 0)
            def _():
                for n, yy in groups(stage - 1):
                    for q in range(NX):
                        high_copy(n, yy, q).wait_recv()

    factor = math.log2(math.e) / math.sqrt(NOPE + ROPE)
    keys = NZH * rows

    def attend(yy):
        first = block_of(yy, 0)
        parts = [all_ref[first + j] for j in range(NZH)]
        compact = jnp.concatenate([p[:LATENT] for p in parts], axis=1)
        rotary = jnp.concatenate([p[LATENT:] for p in parts], axis=1)
        ids = lax.broadcasted_iota(jnp.int32, (2 * NCTX, keys), 0)
        lane = lax.broadcasted_iota(jnp.int32, (2 * NCTX, keys), 1)
        source = first + lane // rows
        key_block = jnp.where(lane % rows < rows // 2, source, 2 * NCTX - 1 - source)
        which = jnp.where(ids == key_block, MASKED, 0.0).astype(BF16)
        for h in range(heads):
            key = jnp.dot(wkt[h], compact, preferred_element_type=F32).astype(BF16)
            value = jnp.dot(wvt[h], compact, preferred_element_type=F32).astype(BF16)
            full = jnp.concatenate([key, rotary, which], axis=0)
            s = jnp.dot(qaug[h], full, preferred_element_type=F32) + diag[...]
            m_old = m_ref[h]
            m_new = jnp.maximum(m_old, jnp.max(s, axis=1, keepdims=True))
            alpha = jnp.exp2((m_old - m_new) * factor)
            p = jnp.exp2((s - m_new[:, :1]) * factor)
            l_ref[h] = l_ref[h] * alpha + jnp.sum(p, axis=1, keepdims=True)
            acc_ref[h] = acc_ref[h] * alpha + nt_dot(p.astype(BF16), value)
            m_ref[h] = m_new

    @pl.loop(0, 6)
    def _(stage):
        @pl.when(stage == 0)
        def _():
            first_duties()

        for v in range(1, 6):
            @pl.when(stage == v)
            def _():
                duties(v)

        step = jnp.maximum(stage - 1, 0)
        count = jnp.where(stage == 1, 0, jnp.where((stage == 0) | (stage == 5), 1, 2))

        @pl.loop(0, 2)
        def _(i):
            @pl.when(i < count)
            def _():
                attend(y + (2 * i - 1) * step)

    for h in range(heads):
        blocks[core, y, :, h * VHEAD : (h + 1) * VHEAD] = (acc_ref[h] / l_ref[h]).astype(BF16)

    def at(yy):
        return lax.rem(yy + NY, NY)

    def a_copy(going_up, step, t, wait):
        off = step if wait else step - 1
        yy = at(y - off if going_up else y + off)
        ref = blocks.at[core, yy, pl.ds(t * (rows // 2), rows // 2), :]
        send, recv, dev = (ar_send, ar_recv, up) if going_up else (al_send, al_recv, down)
        return remote(ref, ref, send.at[step - 1, t], recv.at[step - 1, t], dev)

    def a_goes(going_up, step, t):
        return step < 4 or (step == 4 and (t == 0) == going_up)

    def a_step(step):
        for t in range(2):
            for going_up in (True, False):
                if a_goes(going_up, step, t):
                    if step > 0:
                        a_copy(going_up, step, t, True).wait_recv()
                    if a_goes(going_up, step + 1, t):
                        a_copy(going_up, step + 1, t, False).start()

    def a_sib(n, yy, here):
        ref = blocks.at[core if here else 1 - core, at(yy)]
        return remote(ref, ref, as_send.at[n], as_recv.at[n], sibling)

    def piece_copy(yy):
        return remote(
            outgoing.at[yy], incoming.at[chip], p_send.at[yy], p_recv.at[chip], (me, yy * NCORE + core)
        )

    cols = wo_ref.shape[0]

    def piece(n, yy):
        a_sib(n, yy, False).wait_recv()
        yy = at(yy)
        for r in range(2):
            acc = nt_dot(wog_ref[r, 0], blocks[0, yy]) + nt_dot(wog_ref[r, 1], blocks[1, yy])

            @pl.when(yy == chip)
            def _():
                kept[r * cols : (r + 1) * cols, :] = acc

            @pl.when(yy != chip)
            def _():
                outgoing[yy, r * cols : (r + 1) * cols, :] = acc.astype(BF16)

        @pl.when(yy != chip)
        def _():
            piece_copy(yy).start()

    a_step(0)
    a_sib(0, y, True).start()
    @pl.when(wo_here)
    def _():
        wo_stay.wait()

    for r in range(2):
        for s in range(NCORE):
            @pl.when(jnp.logical_not((k == 2 * core + r) & (core == s)))
            def _():
                ref = wog_ref.at[r, s]
                remote(ref, ref, wo_send.at[0], wo_recv.at[r, s], sibling).wait_recv()

    piece(0, y)
    for step in (1, 2, 3):
        a_step(step)
        a_sib(2 * step - 1, y - step, True).start()
        a_sib(2 * step, y + step, True).start()
        piece(2 * step - 1, y - step)
        piece(2 * step, y + step)
    a_step(4)
    a_sib(7, y + 4, True).start()
    piece(7, y + 4)

    total = kept[...]
    for j in range(1, NCHIP):
        source = lax.rem(chip + j, NCHIP)
        ref = incoming.at[source]
        remote(ref, ref, p_send.at[0], p_recv.at[source], chips[j - 1]).wait_recv()
        total += incoming[source].astype(F32)

    @pl.when(jnp.logical_not(moves))
    def _():
        out_ref[...] = total.astype(BF16)

    @pl.when(moves)
    def _():
        final[...] = total.astype(BF16)
        copy = remote(final, out_ref, f_send, f_recv, last)
        copy.start()
        copy.wait()

    for j in (1, 2, 3):
        z_copy(j).wait_send()
        z_sib(j, True).wait_send()
    for copy in wo_far:
        copy.wait_send()

    @pl.when(jnp.logical_not(wo_here))
    def _():
        wo_pass.wait_send()

    def ring_sent(row0, count):
        for step in (1, 2, 3, 4):
            for j in range(NZH):
                for going_up in (True, False):
                    if goes(going_up, step, j):
                        ring_copy(going_up, step, j, row0, count, False).wait_send()

    @pl.when(core == 0)
    def _():
        ring_sent(0, half)
        for step in (1, 2, 3, 4):
            for n, yy in groups(step):
                low_copy(n, yy).wait_send()

    @pl.when(core == 1)
    def _():
        ring_sent(mine, quarter)
        for step in (1, 2, 3, 4):
            for n, yy in groups(step):
                for q in (1, 2, 3):
                    x_copy(n, yy, q).wait_send()
                for q in range(NX):
                    high_copy(n, yy, q).wait_send()

    for step in (1, 2, 3, 4):
        for t in range(2):
            for going_up in (True, False):
                if a_goes(going_up, step, t):
                    a_copy(going_up, step, t, False).wait_send()
    for n, off in enumerate((0, -1, 1, -2, 2, -3, 3, 4)):
        a_sib(n, y + off, True).wait_send()
    for j in range(1, NCHIP):
        piece_copy(lax.rem(chip + j, NCHIP)).wait_send()


def on_device(query, latent, w_uk, w_uv, w_o, visible):
    rows, width = latent.shape
    inner, cols = w_o.shape
    heads = w_uk.shape[1] // NOPE
    dma = pltpu.SemaphoreType.DMA
    vmem = pltpu.VMEM
    out = pl.pallas_call(
        layer_kernel,
        out_shape=jax.ShapeDtypeStruct((2 * cols, rows), BF16),
        in_specs=[pl.BlockSpec(memory_space=pl.ANY)] * 6,
        out_specs=pl.BlockSpec(memory_space=pltpu.VMEM),
        scratch_shapes=[
            vmem(query.shape, BF16),
            vmem((width, rows), BF16),
            vmem(w_uk.shape, BF16),
            vmem(w_uv.shape, BF16),
            vmem((cols, inner), BF16),
            vmem(visible.shape, jnp.int32),
            vmem((NCTX, width, rows), BF16),
            vmem((2, NCORE, cols, inner), BF16),
            vmem((heads, NOPE, LATENT), BF16),
            vmem((heads, VHEAD, LATENT), BF16),
            vmem((heads, rows, NOPE + ROPE + 2 * NCTX), BF16),
            vmem((rows, NZH * rows), F32),
            vmem((heads, rows, 128), F32),
            vmem((heads, rows, 128), F32),
            vmem((heads, rows, VHEAD), F32),
            vmem((NCORE, NY, rows, inner), BF16),
            vmem((NCHIP, 2 * cols, rows), BF16),
            vmem((NCHIP, 2 * cols, rows), BF16),
            vmem((2 * cols, rows), F32),
            vmem((2 * cols, rows), BF16),
            dma((6,)),
            dma((3,)),
            dma((3,)),
            dma((4, NZH)),
            dma((4, NZH)),
            dma((4, NZH)),
            dma((4, NZH)),
            dma((7, NX)),
            dma((7, NX)),
            dma((4 + 7 * NX,)),
            dma((4 + 7 * NX,)),
            dma((4,)),
            dma((2, NCORE)),
            dma((4, 2)),
            dma((4, 2)),
            dma((4, 2)),
            dma((4, 2)),
            dma((NY,)),
            dma((NY,)),
            dma((NCHIP,)),
            dma((NCHIP,)),
            dma,
            dma,
        ],
        compiler_params=pltpu.CompilerParams(
            collective_id=0, has_side_effects=True, vmem_limit_bytes=56 << 20
        ),
        name="layer",
    )(query, latent.T, w_uk, w_uv, w_o.T, visible)
    return out.T


def solution(mesh):
    in_specs = (P("ctx", "hg"), P("ctx", None), P(None, "hg"), P(None, "hg"), P("hg", "ctx"), P())
    out_specs = P("ctx", "hg")
    return jax.shard_map(
        on_device, mesh=mesh, in_specs=in_specs, out_specs=out_specs, check_vma=False
    )
```

```python
import math

import jax
import jax.numpy as jnp
from jax import lax
from jax.experimental import pallas as pl
from jax.experimental.pallas import tpu as pltpu
from jax.sharding import PartitionSpec as P

NOPE = 128
ROPE = 64
LATENT = 512
VHEAD = 128
NY, NZH, NZL, NX, NCORE = 8, 4, 2, 4, 2
NCTX = NY * NZH
NCHIP = NZL * NX
MESH = pl.DeviceIdType.MESH
MASKED = -1e30
LOW = 224
BF16 = jnp.bfloat16
F32 = jnp.float32


def place():
    c = lax.axis_index("ctx")
    h = lax.axis_index("hg")
    y, k = c // NZH, c % NZH
    chip, core = h // NCORE, h % NCORE
    zl, x = chip // NX, chip % NX
    return y, k, zl, x, core


def device(y, k, zl, x, core):
    return (
        lax.rem(y + NY, NY) * NZH + lax.rem(k + NZH, NZH),
        (zl * NX + lax.rem(x + NX, NX)) * NCORE + core,
    )


def block_of(y, k):
    return lax.rem(y + NY, NY) * NZH + lax.rem(k + NZH, NZH)


def remote(src, dst, send, recv, dev):
    return pltpu.make_async_remote_copy(
        src_ref=src, dst_ref=dst, send_sem=send, recv_sem=recv, device_id=dev, device_id_type=MESH
    )


def nt_dot(a, b):
    return lax.dot_general(a, b, (((1,), (1,)), ((), ())), preferred_element_type=F32)


def layer_kernel(
    q_hbm,
    lat_hbm,
    wk_hbm,
    wv_hbm,
    wo_hbm,
    vis_hbm,
    out_ref,
    q_ref,
    lat_ref,
    wk_ref,
    wv_ref,
    wo_ref,
    vis_ref,
    all_ref,
    wog_ref,
    wkv,
    kv,
    qaug,
    diag,
    m_ref,
    acc_ref,
    blocks,
    outgoing,
    incoming,
    kept,
    final,
    in_sem,
    z_send,
    z_recv,
    r_send,
    r_recv,
    l_send,
    l_recv,
    x_send,
    x_recv,
    sib_send,
    sib_recv,
    wo_send,
    wo_recv,
    wof_send,
    wof_recv,
    ar_send,
    ar_recv,
    al_send,
    al_recv,
    as_send,
    as_recv,
    p_send,
    p_recv,
    f_send,
    f_recv,
):
    y, k, zl, x, core = place()
    chip = zl * NX + x
    width, rows = lat_ref.shape
    heads = acc_ref.shape[0]
    low = LOW
    high = width - low
    quarter = high // NX
    d = 2 * zl - 1
    me = y * NZH + k
    sibling = device(y, k, zl, x, 1 - core)
    line = [device(y, k + j, zl, x, core) for j in (1, 2, 3)]
    line += [device(y, k + j, zl, x, 1 - core) for j in range(NZH)]
    z_targets = [
        device(y, k + d, 1 - zl, x, core),
        device(y, k + d, zl, x, core),
        device(y, k + 2, 1 - zl, x, core),
    ]
    up, down = device(y + 1, k, zl, x, core), device(y - 1, k, zl, x, core)
    x_peers = [device(y, k, zl, x + j, core) for j in (1, 2, 3)]
    chips = [(me, lax.rem(chip + j, NCHIP) * NCORE + core) for j in range(1, NCHIP)]
    mine_y = lax.rem(chip - y + NY, NY)
    last = (mine_y * NZH + k, y * NCORE + core)
    origin = (chip * NZH + k, lax.rem(y + chip, NCHIP) * NCORE + core)
    moves = (chip != y) | (mine_y != y)

    loads = [
        pltpu.make_async_copy(src, dst, in_sem.at[i])
        for i, (src, dst) in enumerate(
            (
                (lat_hbm, lat_ref),
                (q_hbm, q_ref),
                (vis_hbm, vis_ref),
                (wk_hbm, wk_ref),
                (wv_hbm, wv_ref),
                (wo_hbm, wo_ref),
            )
        )
    ]
    for load in loads:
        load.start()

    partners = line + [z_targets[0], z_targets[2], up, down] + chips
    barrier = pltpu.get_barrier_semaphore()
    for dev in partners:
        pl.semaphore_signal(barrier, inc=1, device_id=dev, device_id_type=MESH)

    @pl.when(moves)
    def _():
        pl.semaphore_signal(barrier, inc=1, device_id=origin, device_id_type=MESH)

    pl.semaphore_wait(barrier, len(partners) + jnp.where(moves, 1, 0))

    loads[0].wait()
    parts_of = (pl.ds(0, low), pl.ds(low, high))
    order = [k, k + d, k - d, k + 2]
    mine = pl.multiple_of(low + x * quarter, 8)

    def on_core(visit):
        for c in range(NCORE):
            @pl.when(core == c)
            def _():
                visit(c)

    def z_copy(c, j):
        src, dst = lat_ref.at[parts_of[c], :], all_ref.at[me, parts_of[c], :]
        return remote(src, dst, z_send.at[j - 1], z_recv.at[j - 1], z_targets[j - 1])

    def z_start(c):
        for j in (1, 2, 3):
            z_copy(c, j).start()

    on_core(z_start)
    all_ref[me] = lat_ref[...]

    def z_sib(c, j):
        ref = all_ref.at[block_of(y, order[j]), parts_of[c], :]
        return remote(ref, ref, sib_send.at[j], sib_recv.at[j], sibling)

    def z_pass(j):
        def visit(c):
            ref = all_ref.at[block_of(y, order[j]), parts_of[c], :]
            remote(ref, ref, z_send.at[j - 1], z_recv.at[j - 1], z_targets[j - 1]).wait_recv()
            z_sib(c, j).start()

        on_core(visit)
        ring_start(j)

    def z_sib_wait(c):
        for j in (1, 2, 3):
            z_sib(1 - c, j).wait_recv()

    def ring_copy(going_up, step, j, row0, count, wait):
        off = step if wait else step - 1
        yy = y - off if going_up else y + off
        ref = all_ref.at[block_of(yy, order[j]), pl.ds(row0, count), :]
        send, recv, dev = (r_send, r_recv, up) if going_up else (l_send, l_recv, down)
        return remote(ref, ref, send.at[step - 1, j], recv.at[step - 1, j], dev)

    def goes(going_up, step, j):
        return step < 4 or (step == 4 and (j < 2) == going_up)

    def ring_move(step, blocks_moved):
        def visit(c):
            span = ((0, low), (mine, quarter))[c]
            for j in blocks_moved:
                for going_up in (True, False):
                    if goes(going_up, step, j):
                        ring_copy(going_up, step, j, *span, True).wait_recv()
                        if goes(going_up, step + 1, j):
                            ring_copy(going_up, step + 1, j, *span, False).start()

        on_core(visit)

    def groups(step):
        if step == 4:
            return [(6, y - 4)]
        return [(2 * step - 2, y - step), (2 * step - 1, y + step)]

    def group(yy, row0, count):
        return all_ref.at[pl.ds(block_of(yy, 0), NZH), pl.ds(row0, count), :]

    def low_copy(n, yy):
        ref = group(yy, 0, low)
        return remote(ref, ref, sib_send.at[4 + n * NX], sib_recv.at[4 + n * NX], sibling)

    def high_copy(n, yy, q):
        ref = group(yy, pl.multiple_of(low + lax.rem(x + q, NX) * quarter, 8), quarter)
        slot = 4 + n * NX + q
        return remote(ref, ref, sib_send.at[slot], sib_recv.at[slot], sibling)

    def x_copy(n, yy, q):
        ref = group(yy, mine, quarter)
        return remote(ref, ref, x_send.at[n, q], x_recv.at[n, q], x_peers[q - 1])

    def x_wait(n, yy, q):
        ref = group(yy, pl.multiple_of(low + lax.rem(x + q, NX) * quarter, 8), quarter)
        remote(ref, ref, x_send.at[n, NX - q], x_recv.at[n, NX - q], x_peers[q - 1]).wait_recv()

    def ring_start(j):
        @pl.when(core == 0)
        def _():
            ring_copy(True, 1, j, 0, low, False).start()
            ring_copy(False, 1, j, 0, low, False).start()

        @pl.when(core == 1)
        def _():
            ring_copy(True, 1, j, mine, quarter, False).start()
            ring_copy(False, 1, j, mine, quarter, False).start()

    ring_start(0)

    wo_slot = wog_ref.at[core, k % 2]
    wo_here = core == k // 2
    wo_stay = pltpu.make_async_copy(wo_ref, wo_slot, wo_send.at[0])
    wo_pass = remote(wo_ref, wo_slot, wo_send.at[0], wo_recv.at[core, k % 2], sibling)
    wo_far = [
        remote(wo_ref, wo_slot, wo_send.at[j], wo_recv.at[core, k % 2], device(y, k + j, zl, x, k // 2))
        for j in (1, 3)
    ]
    side = jnp.where(lax.rem(k + 1, NZH) // 2 == core, 1, -1)
    wo_half = wo_ref.shape[0] // 2

    def wo_direct(s):
        ref = wog_ref.at[s, (k + 1) % 2]
        return remote(ref, ref, wo_send.at[0], wo_recv.at[s, (k + 1) % 2], sibling)

    def wo_onward(s):
        first = (1 + side) // 2
        ref = wog_ref.at[s, (k + 1) % 2, pl.ds(pl.multiple_of(first * wo_half, 8), wo_half), :]
        return remote(ref, ref, wof_send.at[s], wof_recv.at[s, first], device(y, k - side, zl, x, core))

    def wo_forward():
        for s in range(NCORE):
            wo_direct(s).wait_recv()
            wo_onward(s).start()

    def wo_arrived():
        @pl.when(wo_here)
        def _():
            wo_stay.wait()
            ref = wog_ref.at[1 - core, k % 2]
            remote(ref, ref, wo_send.at[0], wo_recv.at[1 - core, k % 2], sibling).wait_recv()

        @pl.when(jnp.logical_not(wo_here))
        def _():
            for s in range(NCORE):
                for first in range(2):
                    ref = wog_ref.at[s, k % 2, pl.ds(first * wo_half, wo_half), :]
                    remote(ref, ref, wof_send.at[s], wof_recv.at[s, first], sibling).wait_recv()

    def first_duties():
        for load in loads[1:]:
            load.wait()
        kdim = heads * NOPE
        wkv[:kdim] = wk_ref[...].astype(F32).T.astype(BF16)
        ring_move(1, (0,))
        z_pass(1)
        wkv[kdim:] = wv_ref[...].astype(F32).T.astype(BF16)
        seen = [vis_ref[pl.ds(me, 1), :], vis_ref[pl.ds(2 * NCTX - 1 - me, 1), :]]
        hidden = jnp.concatenate(
            [jnp.broadcast_to(jnp.where(row == 1, 0.0, 1.0), (rows // 2, row.shape[1])) for row in seen], axis=0
        ).astype(BF16)
        for h in range(heads):
            lo = h * (NOPE + ROPE)
            qaug[h] = jnp.concatenate([q_ref[:, lo : lo + NOPE + ROPE], hidden], axis=1)
        i = lax.broadcasted_iota(jnp.int32, diag.shape, 0)
        j = lax.broadcasted_iota(jnp.int32, diag.shape, 1)
        jj = j % rows
        same = (j // rows == k) & (i // (rows // 2) == jj // (rows // 2))
        diag[...] = jnp.where(same & (jj > i), MASKED, 0.0)
        m_ref[...] = jnp.full(m_ref.shape, MASKED, F32)
        acc_ref[...] = jnp.zeros(acc_ref.shape, F32)
        ring_move(2, (0,))
        z_pass(2)
        z_pass(3)
        for copy in wo_far:
            copy.start()

        @pl.when(wo_here)
        def _():
            wo_stay.start()

        @pl.when(jnp.logical_not(wo_here))
        def _():
            wo_pass.start()

        on_core(z_sib_wait)

    def duties(stage):
        if stage <= 4:
            ring_move(stage, range(NZH) if stage == 4 else range(1, NZH))

            @pl.when(core == 0)
            def _():
                for n, yy in groups(stage):
                    low_copy(n, yy).start()

            @pl.when(core == 1)
            def _():
                for n, yy in groups(stage):
                    for q in (1, 2, 3):
                        x_copy(n, yy, q).start()
                    high_copy(n, yy, 0).start()

        if stage == 1:
            ring_move(3, (0,))
        if stage == 3:
            wo_forward()
        if stage == 1:
            diag[...] = jnp.zeros(diag.shape, F32)
        else:
            @pl.when(core == 1)
            def _():
                for n, yy in groups(stage - 1):
                    for q in (1, 2, 3):
                        x_wait(n, yy, q)
                        high_copy(n, yy, q).start()
                for n, yy in groups(stage - 1):
                    low_copy(n, yy).wait_recv()

            @pl.when(core == 0)
            def _():
                for n, yy in groups(stage - 1):
                    for q in range(NX):
                        high_copy(n, yy, q).wait_recv()

    factor = math.log2(math.e) / math.sqrt(NOPE + ROPE)
    keys = NZH * rows

    def attend(yy):
        first = block_of(yy, 0)
        parts = [all_ref[first + j] for j in range(NZH)]
        compact = jnp.concatenate([p[:LATENT] for p in parts], axis=1)
        rotary = jnp.concatenate([p[LATENT:] for p in parts], axis=1)
        ids = lax.broadcasted_iota(jnp.int32, (2 * NCTX, keys), 0)
        lane = lax.broadcasted_iota(jnp.int32, (2 * NCTX, keys), 1)
        source = first + lane // rows
        key_block = jnp.where(lane % rows < rows // 2, source, 2 * NCTX - 1 - source)
        which = jnp.where(ids == key_block, MASKED, 0.0).astype(BF16)
        kv[...] = jnp.dot(wkv[...], compact, preferred_element_type=F32).astype(BF16)
        ones = jnp.ones((VHEAD, keys), BF16)
        for h in range(heads):
            key = kv[h * NOPE : (h + 1) * NOPE]
            value = kv[heads * NOPE + h * VHEAD : heads * NOPE + (h + 1) * VHEAD]
            full = jnp.concatenate([key, rotary, which], axis=0)
            s = jnp.dot(qaug[h], full, preferred_element_type=F32) + diag[...]
            m_old = m_ref[h]
            m_new = jnp.maximum(m_old, jnp.max(s, axis=1, keepdims=True))
            alpha = jnp.exp2((m_old - m_new) * factor)
            p = jnp.exp2((s - m_new[:, :1]) * factor).astype(BF16)
            new = nt_dot(p, jnp.concatenate([value, ones], axis=0))
            acc_ref[h] = acc_ref[h] * jnp.concatenate([alpha, alpha], axis=1) + new
            m_ref[h] = m_new

    @pl.loop(0, 6)
    def _(stage):
        @pl.when(stage == 0)
        def _():
            first_duties()

        for v in range(1, 6):
            @pl.when(stage == v)
            def _():
                duties(v)

        step = jnp.maximum(stage - 1, 0)
        count = jnp.where(stage == 1, 0, jnp.where((stage == 0) | (stage == 5), 1, 2))

        @pl.loop(0, 2)
        def _(i):
            @pl.when(i < count)
            def _():
                attend(y + (2 * i - 1) * step)

    for h in range(heads):
        blocks[core, y, :, h * VHEAD : (h + 1) * VHEAD] = (
            acc_ref[h, :, :VHEAD] / acc_ref[h, :, VHEAD:]
        ).astype(BF16)

    def at(yy):
        return lax.rem(yy + NY, NY)

    def a_copy(going_up, step, t, wait):
        off = step if wait else step - 1
        yy = at(y - off if going_up else y + off)
        ref = blocks.at[core, yy, pl.ds(t * (rows // 2), rows // 2), :]
        send, recv, dev = (ar_send, ar_recv, up) if going_up else (al_send, al_recv, down)
        return remote(ref, ref, send.at[step - 1, t], recv.at[step - 1, t], dev)

    def a_goes(going_up, step, t):
        return step < 4 or (step == 4 and (t == 0) == going_up)

    def a_step(step):
        for t in range(2):
            for going_up in (True, False):
                if a_goes(going_up, step, t):
                    if step > 0:
                        a_copy(going_up, step, t, True).wait_recv()
                    if a_goes(going_up, step + 1, t):
                        a_copy(going_up, step + 1, t, False).start()

    def a_sib(n, yy, here):
        ref = blocks.at[core if here else 1 - core, at(yy)]
        return remote(ref, ref, as_send.at[n], as_recv.at[n], sibling)

    def piece_copy(yy):
        there = (me, lax.rem(y + yy, NCHIP) * NCORE + core)
        return remote(outgoing.at[yy], incoming.at[chip], p_send.at[yy], p_recv.at[chip], there)

    def piece(n, yy):
        a_sib(n, yy, False).wait_recv()
        yy = at(yy)
        acc = nt_dot(wog_ref[0].reshape(out_ref.shape[0], -1), blocks[0, yy])
        acc += nt_dot(wog_ref[1].reshape(out_ref.shape[0], -1), blocks[1, yy])

        @pl.when(yy == mine_y)
        def _():
            kept[...] = acc

        @pl.when(yy != mine_y)
        def _():
            outgoing[yy] = acc.astype(BF16)

        @pl.when(yy != mine_y)
        def _():
            piece_copy(yy).start()

    a_step(0)
    a_sib(0, y, True).start()
    wo_arrived()
    piece(0, y)
    for step in (1, 2, 3):
        a_step(step)
        a_sib(2 * step - 1, y - step, True).start()
        a_sib(2 * step, y + step, True).start()
        piece(2 * step - 1, y - step)
        piece(2 * step, y + step)
    a_step(4)
    a_sib(7, y + 4, True).start()
    piece(7, y + 4)

    total = kept[...]
    for j in range(1, NCHIP):
        source = lax.rem(chip + j, NCHIP)
        ref = incoming.at[source]
        remote(ref, ref, p_send.at[0], p_recv.at[source], chips[j - 1]).wait_recv()
        total += incoming[source].astype(F32)

    @pl.when(jnp.logical_not(moves))
    def _():
        out_ref[...] = total.astype(BF16)

    @pl.when(moves)
    def _():
        final[...] = total.astype(BF16)
        copy = remote(final, out_ref, f_send, f_recv, last)
        copy.start()
        copy.wait()

    def z_sent(c):
        for j in (1, 2, 3):
            z_copy(c, j).wait_send()
            z_sib(c, j).wait_send()

    on_core(z_sent)
    for copy in wo_far:
        copy.wait_send()
    for s in range(NCORE):
        wo_onward(s).wait_send()

    @pl.when(jnp.logical_not(wo_here))
    def _():
        wo_pass.wait_send()

    def ring_sent(row0, count):
        for step in (1, 2, 3, 4):
            for j in range(NZH):
                for going_up in (True, False):
                    if goes(going_up, step, j):
                        ring_copy(going_up, step, j, row0, count, False).wait_send()

    @pl.when(core == 0)
    def _():
        ring_sent(0, low)
        for step in (1, 2, 3, 4):
            for n, yy in groups(step):
                low_copy(n, yy).wait_send()

    @pl.when(core == 1)
    def _():
        ring_sent(mine, quarter)
        for step in (1, 2, 3, 4):
            for n, yy in groups(step):
                for q in (1, 2, 3):
                    x_copy(n, yy, q).wait_send()
                for q in range(NX):
                    high_copy(n, yy, q).wait_send()

    for step in (1, 2, 3, 4):
        for t in range(2):
            for going_up in (True, False):
                if a_goes(going_up, step, t):
                    a_copy(going_up, step, t, False).wait_send()
    for n, off in enumerate((0, -1, 1, -2, 2, -3, 3, 4)):
        a_sib(n, y + off, True).wait_send()
    for j in range(1, NCHIP):
        piece_copy(lax.rem(mine_y + j, NY)).wait_send()


def on_device(query, latent, w_uk, w_uv, w_o, visible):
    rows, width = latent.shape
    inner, cols = w_o.shape
    heads = w_uk.shape[1] // NOPE
    dma = pltpu.SemaphoreType.DMA
    vmem = pltpu.VMEM
    out = pl.pallas_call(
        layer_kernel,
        out_shape=jax.ShapeDtypeStruct((2 * cols, rows), BF16),
        in_specs=[pl.BlockSpec(memory_space=pl.ANY)] * 6,
        out_specs=pl.BlockSpec(memory_space=pltpu.VMEM),
        scratch_shapes=[
            vmem(query.shape, BF16),
            vmem((width, rows), BF16),
            vmem(w_uk.shape, BF16),
            vmem(w_uv.shape, BF16),
            vmem((cols, inner), BF16),
            vmem(visible.shape, jnp.int32),
            vmem((NCTX, width, rows), BF16),
            vmem((NCORE, 2, cols, inner), BF16),
            vmem((heads * (NOPE + VHEAD), LATENT), BF16),
            vmem((heads * (NOPE + VHEAD), NZH * rows), BF16),
            vmem((heads, rows, NOPE + ROPE + 2 * NCTX), BF16),
            vmem((rows, NZH * rows), F32),
            vmem((heads, rows, 128), F32),
            vmem((heads, rows, 2 * VHEAD), F32),
            vmem((NCORE, NY, rows, inner), BF16),
            vmem((NCHIP, 2 * cols, rows), BF16),
            vmem((NCHIP, 2 * cols, rows), BF16),
            vmem((2 * cols, rows), F32),
            vmem((2 * cols, rows), BF16),
            dma((6,)),
            dma((3,)),
            dma((3,)),
            dma((4, NZH)),
            dma((4, NZH)),
            dma((4, NZH)),
            dma((4, NZH)),
            dma((7, NX)),
            dma((7, NX)),
            dma((4 + 7 * NX,)),
            dma((4 + 7 * NX,)),
            dma((4,)),
            dma((NCORE, 2)),
            dma((NCORE,)),
            dma((NCORE, 2)),
            dma((4, 2)),
            dma((4, 2)),
            dma((4, 2)),
            dma((4, 2)),
            dma((NY,)),
            dma((NY,)),
            dma((NCHIP,)),
            dma((NCHIP,)),
            dma,
            dma,
        ],
        compiler_params=pltpu.CompilerParams(
            collective_id=0, has_side_effects=True, vmem_limit_bytes=56 << 20
        ),
        name="layer",
    )(query, latent.T, w_uk, w_uv, w_o.T, visible)
    return out.T


def solution(mesh):
    in_specs = (P("ctx", "hg"), P("ctx", None), P(None, "hg"), P(None, "hg"), P("hg", "ctx"), P())
    out_specs = P("ctx", "hg")
    return jax.shard_map(
        on_device, mesh=mesh, in_specs=in_specs, out_specs=out_specs, check_vma=False
    )
```

```python
import math

import jax
import jax.numpy as jnp
from jax import lax
from jax.experimental import pallas as pl
from jax.experimental.pallas import tpu as pltpu
from jax.sharding import PartitionSpec as P

NOPE = 128
ROPE = 64
LATENT = 512
VHEAD = 128
NY, NZH, NZL, NX, NCORE = 8, 4, 2, 4, 2
NCTX = NY * NZH
NCHIP = NZL * NX
MESH = pl.DeviceIdType.MESH
MASKED = -1e30
LOW = 224
BF16 = jnp.bfloat16
F32 = jnp.float32


def place():
    c = lax.axis_index("ctx")
    h = lax.axis_index("hg")
    y, k = c // NZH, c % NZH
    chip, core = h // NCORE, h % NCORE
    zl, x = chip // NX, chip % NX
    return y, k, zl, x, core


def device(y, k, zl, x, core):
    return (
        lax.rem(y + NY, NY) * NZH + lax.rem(k + NZH, NZH),
        (zl * NX + lax.rem(x + NX, NX)) * NCORE + core,
    )


def block_of(y, k):
    return lax.rem(y + NY, NY) * NZH + lax.rem(k + NZH, NZH)


def remote(src, dst, send, recv, dev):
    return pltpu.make_async_remote_copy(
        src_ref=src, dst_ref=dst, send_sem=send, recv_sem=recv, device_id=dev, device_id_type=MESH
    )


def nt_dot(a, b):
    return lax.dot_general(a, b, (((1,), (1,)), ((), ())), preferred_element_type=F32)


def layer_kernel(
    q_hbm,
    lat_hbm,
    wk_hbm,
    wv_hbm,
    wo_hbm,
    vis_hbm,
    out_ref,
    q_ref,
    lat_ref,
    wk_ref,
    wv_ref,
    wo_ref,
    vis_ref,
    all_ref,
    wog_ref,
    wkv,
    kv,
    qaug,
    diag,
    m_ref,
    acc_ref,
    blocks,
    outgoing,
    incoming,
    kept,
    final,
    in_sem,
    z_send,
    z_recv,
    r_send,
    r_recv,
    l_send,
    l_recv,
    x_send,
    x_recv,
    sib_send,
    sib_recv,
    wo_send,
    wo_recv,
    wof_send,
    wof_recv,
    ar_send,
    ar_recv,
    al_send,
    al_recv,
    as_send,
    as_recv,
    p_send,
    p_recv,
    f_send,
    f_recv,
):
    y, k, zl, x, core = place()
    chip = zl * NX + x
    width, rows = lat_ref.shape
    heads = acc_ref.shape[0]
    low = LOW
    high = width - low
    quarter = high // NX
    d = 2 * zl - 1
    me = y * NZH + k
    sibling = device(y, k, zl, x, 1 - core)
    line = [device(y, k + j, zl, x, core) for j in (1, 2, 3)]
    line += [device(y, k + j, zl, x, 1 - core) for j in range(NZH)]
    z_targets = [
        device(y, k + d, 1 - zl, x, core),
        device(y, k + d, zl, x, core),
        device(y, k + 2, 1 - zl, x, core),
    ]
    up, down = device(y + 1, k, zl, x, core), device(y - 1, k, zl, x, core)
    x_peers = [device(y, k, zl, x + j, core) for j in (1, 2, 3)]
    chips = [(me, lax.rem(chip + j, NCHIP) * NCORE + core) for j in range(1, NCHIP)]
    mine_y = lax.rem(chip - y + NY, NY)
    last = (mine_y * NZH + k, y * NCORE + core)
    origin = (chip * NZH + k, lax.rem(y + chip, NCHIP) * NCORE + core)
    moves = (chip != y) | (mine_y != y)

    loads = [
        pltpu.make_async_copy(src, dst, in_sem.at[i])
        for i, (src, dst) in enumerate(
            (
                (lat_hbm, lat_ref),
                (q_hbm, q_ref),
                (vis_hbm, vis_ref),
                (wk_hbm, wk_ref),
                (wv_hbm, wv_ref),
                (wo_hbm, wo_ref),
            )
        )
    ]
    for load in loads:
        load.start()

    partners = line + [z_targets[0], z_targets[2], up, down] + chips
    barrier = pltpu.get_barrier_semaphore()
    for dev in partners:
        pl.semaphore_signal(barrier, inc=1, device_id=dev, device_id_type=MESH)

    @pl.when(moves)
    def _():
        pl.semaphore_signal(barrier, inc=1, device_id=origin, device_id_type=MESH)

    pl.semaphore_wait(barrier, len(partners) + jnp.where(moves, 1, 0))

    loads[0].wait()
    parts_of = (pl.ds(0, low), pl.ds(low, high))
    order = [k, k + d, k - d, k + 2]
    mine = pl.multiple_of(low + x * quarter, 8)

    def on_core(visit):
        for c in range(NCORE):
            @pl.when(core == c)
            def _():
                visit(c)

    def z_copy(c, j):
        src, dst = lat_ref.at[parts_of[c], :], all_ref.at[me, parts_of[c], :]
        return remote(src, dst, z_send.at[j - 1], z_recv.at[j - 1], z_targets[j - 1])

    def z_start(c):
        for j in (1, 2, 3):
            z_copy(c, j).start()

    on_core(z_start)
    all_ref[me] = lat_ref[...]

    def z_sib(c, j):
        ref = all_ref.at[block_of(y, order[j]), parts_of[c], :]
        return remote(ref, ref, sib_send.at[j], sib_recv.at[j], sibling)

    def z_pass(j):
        def visit(c):
            ref = all_ref.at[block_of(y, order[j]), parts_of[c], :]
            remote(ref, ref, z_send.at[j - 1], z_recv.at[j - 1], z_targets[j - 1]).wait_recv()
            z_sib(c, j).start()

        on_core(visit)
        ring_start(j)

    def z_sib_wait(c):
        for j in (1, 2, 3):
            z_sib(1 - c, j).wait_recv()

    def ring_copy(going_up, step, j, row0, count, wait):
        off = step if wait else step - 1
        yy = y - off if going_up else y + off
        ref = all_ref.at[block_of(yy, order[j]), pl.ds(row0, count), :]
        send, recv, dev = (r_send, r_recv, up) if going_up else (l_send, l_recv, down)
        return remote(ref, ref, send.at[step - 1, j], recv.at[step - 1, j], dev)

    def goes(going_up, step, j):
        return step < 4 or (step == 4 and (j < 2) == going_up)

    def ring_move(step, blocks_moved):
        def visit(c):
            span = ((0, low), (mine, quarter))[c]
            for j in blocks_moved:
                for going_up in (True, False):
                    if goes(going_up, step, j):
                        ring_copy(going_up, step, j, *span, True).wait_recv()
                        if goes(going_up, step + 1, j):
                            ring_copy(going_up, step + 1, j, *span, False).start()

        on_core(visit)

    def groups(step):
        if step == 4:
            return [(6, y - 4)]
        return [(2 * step - 2, y - step), (2 * step - 1, y + step)]

    def group(yy, row0, count):
        return all_ref.at[pl.ds(block_of(yy, 0), NZH), pl.ds(row0, count), :]

    def low_copy(n, yy):
        ref = group(yy, 0, low)
        return remote(ref, ref, sib_send.at[4 + n * NX], sib_recv.at[4 + n * NX], sibling)

    def high_copy(n, yy, q):
        ref = group(yy, pl.multiple_of(low + lax.rem(x + q, NX) * quarter, 8), quarter)
        slot = 4 + n * NX + q
        return remote(ref, ref, sib_send.at[slot], sib_recv.at[slot], sibling)

    def x_copy(n, yy, q):
        ref = group(yy, mine, quarter)
        return remote(ref, ref, x_send.at[n, q], x_recv.at[n, q], x_peers[q - 1])

    def x_wait(n, yy, q):
        ref = group(yy, pl.multiple_of(low + lax.rem(x + q, NX) * quarter, 8), quarter)
        remote(ref, ref, x_send.at[n, NX - q], x_recv.at[n, NX - q], x_peers[q - 1]).wait_recv()

    def ring_start(j):
        @pl.when(core == 0)
        def _():
            ring_copy(True, 1, j, 0, low, False).start()
            ring_copy(False, 1, j, 0, low, False).start()

        @pl.when(core == 1)
        def _():
            ring_copy(True, 1, j, mine, quarter, False).start()
            ring_copy(False, 1, j, mine, quarter, False).start()

    ring_start(0)

    wo_slot = wog_ref.at[core, k % 2]
    wo_here = core == k // 2
    wo_stay = pltpu.make_async_copy(wo_ref, wo_slot, wo_send.at[0])
    wo_pass = remote(wo_ref, wo_slot, wo_send.at[0], wo_recv.at[core, k % 2], sibling)
    wo_far = [
        remote(wo_ref, wo_slot, wo_send.at[j], wo_recv.at[core, k % 2], device(y, k + j, zl, x, k // 2))
        for j in (1, 3)
    ]
    side = jnp.where(lax.rem(k + 1, NZH) // 2 == core, 1, -1)
    wo_half = wo_ref.shape[0] // 2

    def wo_direct(s):
        ref = wog_ref.at[s, (k + 1) % 2]
        return remote(ref, ref, wo_send.at[0], wo_recv.at[s, (k + 1) % 2], sibling)

    def wo_onward(s):
        first = (1 + side) // 2
        ref = wog_ref.at[s, (k + 1) % 2, pl.ds(pl.multiple_of(first * wo_half, 8), wo_half), :]
        return remote(ref, ref, wof_send.at[s], wof_recv.at[s, first], device(y, k - side, zl, x, core))

    def wo_forward():
        for s in range(NCORE):
            wo_direct(s).wait_recv()
            wo_onward(s).start()

    def wo_arrived():
        @pl.when(wo_here)
        def _():
            wo_stay.wait()
            ref = wog_ref.at[1 - core, k % 2]
            remote(ref, ref, wo_send.at[0], wo_recv.at[1 - core, k % 2], sibling).wait_recv()

        @pl.when(jnp.logical_not(wo_here))
        def _():
            for s in range(NCORE):
                for first in range(2):
                    ref = wog_ref.at[s, k % 2, pl.ds(first * wo_half, wo_half), :]
                    remote(ref, ref, wof_send.at[s], wof_recv.at[s, first], sibling).wait_recv()

    def first_duties():
        for load in loads[1:]:
            load.wait()
        kdim = heads * NOPE
        wkv[:kdim] = wk_ref[...].astype(F32).T.astype(BF16)
        ring_move(1, (0,))
        z_pass(1)
        wkv[kdim:] = wv_ref[...].astype(F32).T.astype(BF16)
        seen = [vis_ref[pl.ds(me, 1), :], vis_ref[pl.ds(2 * NCTX - 1 - me, 1), :]]
        hidden = jnp.concatenate(
            [jnp.broadcast_to(jnp.where(row == 1, 0.0, 1.0), (rows // 2, row.shape[1])) for row in seen], axis=0
        ).astype(BF16)
        for h in range(heads):
            lo = h * (NOPE + ROPE)
            qaug[h] = jnp.concatenate([q_ref[:, lo : lo + NOPE + ROPE], hidden], axis=1)
        i = lax.broadcasted_iota(jnp.int32, diag.shape, 0)
        j = lax.broadcasted_iota(jnp.int32, diag.shape, 1)
        jj = j % rows
        same = (j // rows == k) & (i // (rows // 2) == jj // (rows // 2))
        diag[...] = jnp.where(same & (jj > i), MASKED, 0.0)
        m_ref[...] = jnp.full(m_ref.shape, MASKED, F32)
        acc_ref[...] = jnp.zeros(acc_ref.shape, F32)
        ring_move(2, (0,))
        z_pass(2)
        z_pass(3)
        for copy in wo_far:
            copy.start()

        @pl.when(wo_here)
        def _():
            wo_stay.start()

        @pl.when(jnp.logical_not(wo_here))
        def _():
            wo_pass.start()

        on_core(z_sib_wait)

    def duties(stage):
        if stage <= 4:
            ring_move(stage, range(NZH) if stage == 4 else range(1, NZH))

            @pl.when(core == 0)
            def _():
                for n, yy in groups(stage):
                    low_copy(n, yy).start()

            @pl.when(core == 1)
            def _():
                for n, yy in groups(stage):
                    for q in (1, 2, 3):
                        x_copy(n, yy, q).start()
                    high_copy(n, yy, 0).start()

        if stage == 1:
            ring_move(3, (0,))
        if stage == 3:
            wo_forward()
        if stage == 1:
            diag[...] = jnp.zeros(diag.shape, F32)
        else:
            @pl.when(core == 1)
            def _():
                for n, yy in groups(stage - 1):
                    for q in (1, 2, 3):
                        x_wait(n, yy, q)
                        high_copy(n, yy, q).start()
                for n, yy in groups(stage - 1):
                    low_copy(n, yy).wait_recv()

            @pl.when(core == 0)
            def _():
                for n, yy in groups(stage - 1):
                    for q in range(NX):
                        high_copy(n, yy, q).wait_recv()

    factor = math.log2(math.e) / math.sqrt(NOPE + ROPE)
    keys = NZH * rows

    def attend(groups_now, masked):
        firsts = [block_of(yy, 0) for yy in groups_now]
        parts = [all_ref[first + j] for first in firsts for j in range(NZH)]
        count = keys * len(groups_now)
        ids = lax.broadcasted_iota(jnp.int32, (2 * NCTX, keys), 0)
        lane = lax.broadcasted_iota(jnp.int32, (2 * NCTX, keys), 1)
        tails = []
        for i, first in enumerate(firsts):
            source = first + lane // rows
            key_block = jnp.where(lane % rows < rows // 2, source, 2 * NCTX - 1 - source)
            which = jnp.where(ids == key_block, MASKED, 0.0).astype(BF16)
            rotary = jnp.concatenate([p[LATENT:] for p in parts[NZH * i : NZH * (i + 1)]], axis=1)
            tails.append(jnp.concatenate([rotary, which], axis=0))
        kdim = heads * NOPE
        compacts = [
            jnp.concatenate([p[:LATENT] for p in parts[NZH * i : NZH * (i + 1)]], axis=1)
            for i in range(len(firsts))
        ]

        def expand(i, lo, hi):
            kv[lo:hi, i * keys : (i + 1) * keys] = jnp.dot(
                wkv[lo:hi], compacts[i], preferred_element_type=F32
            ).astype(BF16)

        for i in range(len(firsts)):
            expand(i, 0, kdim)
        tail = jnp.concatenate(tails, axis=1)
        ones = jnp.ones((VHEAD, count), BF16)

        def scores(h):
            full = jnp.concatenate([kv[h * NOPE : (h + 1) * NOPE, :count], tail], axis=0)
            s = jnp.dot(qaug[h], full, preferred_element_type=F32)
            return s + diag[...] if masked else s

        def weigh(h, p, alpha):
            row = (heads + h) * VHEAD
            new = nt_dot(p, jnp.concatenate([kv[row : row + VHEAD, :count], ones], axis=0))
            acc_ref[h] = acc_ref[h] * jnp.concatenate([alpha, alpha], axis=1) + new

        following = scores(0)
        waiting = None
        for h in range(heads):
            s = following
            if h + 1 < heads:
                following = scores(h + 1)
            if h < len(firsts):
                expand(h, kdim, 2 * kdim)
            m_old = m_ref[h]
            m_new = jnp.maximum(m_old, jnp.max(s, axis=1, keepdims=True))
            alpha = jnp.exp2((m_old - m_new) * factor)
            p = jnp.exp2((s - m_new[:, :1]) * factor).astype(BF16)
            m_ref[h] = m_new
            if waiting:
                weigh(*waiting)
            waiting = (h, p, alpha)
        weigh(*waiting)

    @pl.loop(0, 6)
    def _(stage):
        @pl.when(stage == 0)
        def _():
            first_duties()

        for v in range(1, 6):
            @pl.when(stage == v)
            def _():
                duties(v)

        @pl.when((stage == 0) | (stage == 5))
        def _():
            attend([y - jnp.where(stage == 0, 0, 4)], True)

        @pl.when((stage > 1) & (stage < 5))
        def _():
            attend([y - (stage - 1), y + (stage - 1)], False)

    for h in range(heads):
        blocks[core, y, :, h * VHEAD : (h + 1) * VHEAD] = (
            acc_ref[h, :, :VHEAD] / acc_ref[h, :, VHEAD:]
        ).astype(BF16)

    def at(yy):
        return lax.rem(yy + NY, NY)

    def a_copy(going_up, step, t, wait):
        off = step if wait else step - 1
        yy = at(y - off if going_up else y + off)
        ref = blocks.at[core, yy, pl.ds(t * (rows // 2), rows // 2), :]
        send, recv, dev = (ar_send, ar_recv, up) if going_up else (al_send, al_recv, down)
        return remote(ref, ref, send.at[step - 1, t], recv.at[step - 1, t], dev)

    def a_goes(going_up, step, t):
        return step < 4 or (step == 4 and (t == 0) == going_up)

    def a_step(step):
        for t in range(2):
            for going_up in (True, False):
                if a_goes(going_up, step, t):
                    if step > 0:
                        a_copy(going_up, step, t, True).wait_recv()
                    if a_goes(going_up, step + 1, t):
                        a_copy(going_up, step + 1, t, False).start()

    def a_sib(n, yy, here):
        ref = blocks.at[core if here else 1 - core, at(yy)]
        return remote(ref, ref, as_send.at[n], as_recv.at[n], sibling)

    def piece_copy(yy):
        there = (me, lax.rem(y + yy, NCHIP) * NCORE + core)
        return remote(outgoing.at[yy], incoming.at[chip], p_send.at[yy], p_recv.at[chip], there)

    def piece(n, yy):
        a_sib(n, yy, False).wait_recv()
        yy = at(yy)
        acc = nt_dot(wog_ref[0].reshape(out_ref.shape[0], -1), blocks[0, yy])
        acc += nt_dot(wog_ref[1].reshape(out_ref.shape[0], -1), blocks[1, yy])

        @pl.when(yy == mine_y)
        def _():
            kept[...] = acc

        @pl.when(yy != mine_y)
        def _():
            outgoing[yy] = acc.astype(BF16)

        @pl.when(yy != mine_y)
        def _():
            piece_copy(yy).start()

    a_step(0)
    a_sib(0, y, True).start()
    wo_arrived()
    piece(0, y)
    for step in (1, 2, 3):
        a_step(step)
        a_sib(2 * step - 1, y - step, True).start()
        a_sib(2 * step, y + step, True).start()
        piece(2 * step - 1, y - step)
        piece(2 * step, y + step)
    a_step(4)
    a_sib(7, y + 4, True).start()
    piece(7, y + 4)

    total = kept[...]
    for j in range(1, NCHIP):
        source = lax.rem(chip + j, NCHIP)
        ref = incoming.at[source]
        remote(ref, ref, p_send.at[0], p_recv.at[source], chips[j - 1]).wait_recv()
        total += incoming[source].astype(F32)

    @pl.when(jnp.logical_not(moves))
    def _():
        out_ref[...] = total.astype(BF16)

    @pl.when(moves)
    def _():
        final[...] = total.astype(BF16)
        copy = remote(final, out_ref, f_send, f_recv, last)
        copy.start()
        copy.wait()

    def z_sent(c):
        for j in (1, 2, 3):
            z_copy(c, j).wait_send()
            z_sib(c, j).wait_send()

    on_core(z_sent)
    for copy in wo_far:
        copy.wait_send()
    for s in range(NCORE):
        wo_onward(s).wait_send()

    @pl.when(jnp.logical_not(wo_here))
    def _():
        wo_pass.wait_send()

    def ring_sent(row0, count):
        for step in (1, 2, 3, 4):
            for j in range(NZH):
                for going_up in (True, False):
                    if goes(going_up, step, j):
                        ring_copy(going_up, step, j, row0, count, False).wait_send()

    @pl.when(core == 0)
    def _():
        ring_sent(0, low)
        for step in (1, 2, 3, 4):
            for n, yy in groups(step):
                low_copy(n, yy).wait_send()

    @pl.when(core == 1)
    def _():
        ring_sent(mine, quarter)
        for step in (1, 2, 3, 4):
            for n, yy in groups(step):
                for q in (1, 2, 3):
                    x_copy(n, yy, q).wait_send()
                for q in range(NX):
                    high_copy(n, yy, q).wait_send()

    for step in (1, 2, 3, 4):
        for t in range(2):
            for going_up in (True, False):
                if a_goes(going_up, step, t):
                    a_copy(going_up, step, t, False).wait_send()
    for n, off in enumerate((0, -1, 1, -2, 2, -3, 3, 4)):
        a_sib(n, y + off, True).wait_send()
    for j in range(1, NCHIP):
        piece_copy(lax.rem(mine_y + j, NY)).wait_send()


def on_device(query, latent, w_uk, w_uv, w_o, visible):
    rows, width = latent.shape
    inner, cols = w_o.shape
    heads = w_uk.shape[1] // NOPE
    dma = pltpu.SemaphoreType.DMA
    vmem = pltpu.VMEM
    out = pl.pallas_call(
        layer_kernel,
        out_shape=jax.ShapeDtypeStruct((2 * cols, rows), BF16),
        in_specs=[pl.BlockSpec(memory_space=pl.ANY)] * 6,
        out_specs=pl.BlockSpec(memory_space=pltpu.VMEM),
        scratch_shapes=[
            vmem(query.shape, BF16),
            vmem((width, rows), BF16),
            vmem(w_uk.shape, BF16),
            vmem(w_uv.shape, BF16),
            vmem((cols, inner), BF16),
            vmem(visible.shape, jnp.int32),
            vmem((NCTX, width, rows), BF16),
            vmem((NCORE, 2, cols, inner), BF16),
            vmem((heads * (NOPE + VHEAD), LATENT), BF16),
            vmem((heads * (NOPE + VHEAD), 2 * NZH * rows), BF16),
            vmem((heads, rows, NOPE + ROPE + 2 * NCTX), BF16),
            vmem((rows, NZH * rows), F32),
            vmem((heads, rows, 128), F32),
            vmem((heads, rows, 2 * VHEAD), F32),
            vmem((NCORE, NY, rows, inner), BF16),
            vmem((NCHIP, 2 * cols, rows), BF16),
            vmem((NCHIP, 2 * cols, rows), BF16),
            vmem((2 * cols, rows), F32),
            vmem((2 * cols, rows), BF16),
            dma((6,)),
            dma((3,)),
            dma((3,)),
            dma((4, NZH)),
            dma((4, NZH)),
            dma((4, NZH)),
            dma((4, NZH)),
            dma((7, NX)),
            dma((7, NX)),
            dma((4 + 7 * NX,)),
            dma((4 + 7 * NX,)),
            dma((4,)),
            dma((NCORE, 2)),
            dma((NCORE,)),
            dma((NCORE, 2)),
            dma((4, 2)),
            dma((4, 2)),
            dma((4, 2)),
            dma((4, 2)),
            dma((NY,)),
            dma((NY,)),
            dma((NCHIP,)),
            dma((NCHIP,)),
            dma,
            dma,
        ],
        compiler_params=pltpu.CompilerParams(
            collective_id=0, has_side_effects=True, vmem_limit_bytes=56 << 20
        ),
        name="layer",
    )(query, latent.T, w_uk, w_uv, w_o.T, visible)
    return out.T


def solution(mesh):
    in_specs = (P("ctx", "hg"), P("ctx", None), P(None, "hg"), P(None, "hg"), P("hg", "ctx"), P())
    out_specs = P("ctx", "hg")
    return jax.shard_map(
        on_device, mesh=mesh, in_specs=in_specs, out_specs=out_specs, check_vma=False
    )
```

```python
import math

import jax
import jax.numpy as jnp
from jax import lax
from jax.experimental import pallas as pl
from jax.experimental.pallas import tpu as pltpu
from jax.sharding import PartitionSpec as P

NOPE = 128
ROPE = 64
LATENT = 512
VHEAD = 128
NY, NZH, NZL, NX, NCORE = 8, 4, 2, 4, 2
NCTX = NY * NZH
NCHIP = NZL * NX
MESH = pl.DeviceIdType.MESH
MASKED = -1e30
LOW = 224
BF16 = jnp.bfloat16
F32 = jnp.float32


def place():
    c = lax.axis_index("ctx")
    h = lax.axis_index("hg")
    y, k = c // NZH, c % NZH
    chip, core = h // NCORE, h % NCORE
    zl, x = chip // NX, chip % NX
    return y, k, zl, x, core


def device(y, k, zl, x, core):
    return (
        lax.rem(y + NY, NY) * NZH + lax.rem(k + NZH, NZH),
        (zl * NX + lax.rem(x + NX, NX)) * NCORE + core,
    )


def block_of(y, k):
    return lax.rem(y + NY, NY) * NZH + lax.rem(k + NZH, NZH)


def remote(src, dst, send, recv, dev):
    return pltpu.make_async_remote_copy(
        src_ref=src, dst_ref=dst, send_sem=send, recv_sem=recv, device_id=dev, device_id_type=MESH
    )


def nt_dot(a, b):
    return lax.dot_general(a, b, (((1,), (1,)), ((), ())), preferred_element_type=F32)


def layer_kernel(
    q_hbm,
    lat_hbm,
    wk_hbm,
    wv_hbm,
    wo_hbm,
    vis_hbm,
    out_ref,
    q_ref,
    lat_ref,
    wk_ref,
    wv_ref,
    wo_ref,
    vis_ref,
    all_ref,
    wog_ref,
    wkv,
    kv,
    qaug,
    diag,
    m_ref,
    acc_ref,
    blocks,
    outgoing,
    incoming,
    kept,
    final,
    in_sem,
    z_send,
    z_recv,
    r_send,
    r_recv,
    l_send,
    l_recv,
    x_send,
    x_recv,
    sib_send,
    sib_recv,
    wo_send,
    wo_recv,
    wof_send,
    wof_recv,
    ar_send,
    ar_recv,
    al_send,
    al_recv,
    as_send,
    as_recv,
    p_send,
    p_recv,
    f_send,
    f_recv,
):
    y, k, zl, x, core = place()
    chip = zl * NX + x
    width, rows = lat_ref.shape
    heads = acc_ref.shape[0]
    low = LOW
    high = width - low
    quarter = high // NX
    d = 2 * zl - 1
    me = y * NZH + k
    sibling = device(y, k, zl, x, 1 - core)
    line = [device(y, k + j, zl, x, core) for j in (1, 2, 3)]
    line += [device(y, k + j, zl, x, 1 - core) for j in range(NZH)]
    z_targets = [
        device(y, k + d, 1 - zl, x, core),
        device(y, k + d, zl, x, core),
        device(y, k + 2, 1 - zl, x, core),
    ]
    up, down = device(y + 1, k, zl, x, core), device(y - 1, k, zl, x, core)
    x_peers = [device(y, k, zl, x + j, core) for j in (1, 2, 3)]
    chips = [(me, lax.rem(chip + j, NCHIP) * NCORE + core) for j in range(1, NCHIP)]
    mine_y = lax.rem(chip - y + NY, NY)
    last = (mine_y * NZH + k, y * NCORE + core)
    origin = (chip * NZH + k, lax.rem(y + chip, NCHIP) * NCORE + core)
    moves = (chip != y) | (mine_y != y)

    loads = [
        pltpu.make_async_copy(src, dst, in_sem.at[i])
        for i, (src, dst) in enumerate(
            (
                (lat_hbm, lat_ref),
                (q_hbm, q_ref),
                (vis_hbm, vis_ref),
                (wk_hbm, wk_ref),
                (wv_hbm, wv_ref),
                (wo_hbm, wo_ref),
            )
        )
    ]
    for load in loads:
        load.start()

    partners = line + [z_targets[0], z_targets[2], up, down] + chips
    barrier = pltpu.get_barrier_semaphore()
    for dev in partners:
        pl.semaphore_signal(barrier, inc=1, device_id=dev, device_id_type=MESH)

    @pl.when(moves)
    def _():
        pl.semaphore_signal(barrier, inc=1, device_id=origin, device_id_type=MESH)

    pl.semaphore_wait(barrier, len(partners) + jnp.where(moves, 1, 0))

    loads[0].wait()
    parts_of = (pl.ds(0, low), pl.ds(low, high))
    order = [k, k + d, k - d, k + 2]
    mine = pl.multiple_of(low + x * quarter, 8)

    def on_core(visit):
        for c in range(NCORE):
            @pl.when(core == c)
            def _():
                visit(c)

    def z_copy(c, j):
        src, dst = lat_ref.at[parts_of[c], :], all_ref.at[me, parts_of[c], :]
        return remote(src, dst, z_send.at[j - 1], z_recv.at[j - 1], z_targets[j - 1])

    def z_start(c):
        for j in (1, 2, 3):
            z_copy(c, j).start()

    on_core(z_start)
    all_ref[me] = lat_ref[...]

    def z_sib(c, j):
        ref = all_ref.at[block_of(y, order[j]), parts_of[c], :]
        return remote(ref, ref, sib_send.at[j], sib_recv.at[j], sibling)

    def z_pass(j):
        def visit(c):
            ref = all_ref.at[block_of(y, order[j]), parts_of[c], :]
            remote(ref, ref, z_send.at[j - 1], z_recv.at[j - 1], z_targets[j - 1]).wait_recv()
            z_sib(c, j).start()

        on_core(visit)
        ring_start(j)

    def z_sib_wait(c):
        for j in (1, 2, 3):
            z_sib(1 - c, j).wait_recv()

    def ring_copy(going_up, step, j, row0, count, wait):
        off = step if wait else step - 1
        yy = y - off if going_up else y + off
        ref = all_ref.at[block_of(yy, order[j]), pl.ds(row0, count), :]
        send, recv, dev = (r_send, r_recv, up) if going_up else (l_send, l_recv, down)
        return remote(ref, ref, send.at[step - 1, j], recv.at[step - 1, j], dev)

    def goes(going_up, step, j):
        return step < 4 or (step == 4 and (j < 2) == going_up)

    def ring_move(step, blocks_moved):
        def visit(c):
            span = ((0, low), (mine, quarter))[c]
            for j in blocks_moved:
                for going_up in (True, False):
                    if goes(going_up, step, j):
                        ring_copy(going_up, step, j, *span, True).wait_recv()
                        if goes(going_up, step + 1, j):
                            ring_copy(going_up, step + 1, j, *span, False).start()

        on_core(visit)

    def groups(step):
        if step == 4:
            return [(6, y - 4)]
        return [(2 * step - 2, y - step), (2 * step - 1, y + step)]

    def group(yy, row0, count):
        return all_ref.at[pl.ds(block_of(yy, 0), NZH), pl.ds(row0, count), :]

    def low_copy(n, yy):
        ref = group(yy, 0, low)
        return remote(ref, ref, sib_send.at[4 + n * NX], sib_recv.at[4 + n * NX], sibling)

    def high_copy(n, yy, q):
        ref = group(yy, pl.multiple_of(low + lax.rem(x + q, NX) * quarter, 8), quarter)
        slot = 4 + n * NX + q
        return remote(ref, ref, sib_send.at[slot], sib_recv.at[slot], sibling)

    def x_copy(n, yy, q):
        ref = group(yy, mine, quarter)
        return remote(ref, ref, x_send.at[n, q], x_recv.at[n, q], x_peers[q - 1])

    def x_wait(n, yy, q):
        ref = group(yy, pl.multiple_of(low + lax.rem(x + q, NX) * quarter, 8), quarter)
        remote(ref, ref, x_send.at[n, NX - q], x_recv.at[n, NX - q], x_peers[q - 1]).wait_recv()

    def ring_start(j):
        @pl.when(core == 0)
        def _():
            ring_copy(True, 1, j, 0, low, False).start()
            ring_copy(False, 1, j, 0, low, False).start()

        @pl.when(core == 1)
        def _():
            ring_copy(True, 1, j, mine, quarter, False).start()
            ring_copy(False, 1, j, mine, quarter, False).start()

    ring_start(0)

    wo_slot = wog_ref.at[core, k % 2]
    wo_here = core == k // 2
    wo_stay = pltpu.make_async_copy(wo_ref, wo_slot, wo_send.at[0])
    wo_pass = remote(wo_ref, wo_slot, wo_send.at[0], wo_recv.at[core, k % 2], sibling)
    wo_far = [
        remote(wo_ref, wo_slot, wo_send.at[j], wo_recv.at[core, k % 2], device(y, k + j, zl, x, k // 2))
        for j in (1, 3)
    ]
    side = jnp.where(lax.rem(k + 1, NZH) // 2 == core, 1, -1)
    wo_half = wo_ref.shape[0] // 2

    def wo_direct(s):
        ref = wog_ref.at[s, (k + 1) % 2]
        return remote(ref, ref, wo_send.at[0], wo_recv.at[s, (k + 1) % 2], sibling)

    def wo_onward(s):
        first = (1 + side) // 2
        ref = wog_ref.at[s, (k + 1) % 2, pl.ds(pl.multiple_of(first * wo_half, 8), wo_half), :]
        return remote(ref, ref, wof_send.at[s], wof_recv.at[s, first], device(y, k - side, zl, x, core))

    def wo_forward():
        for s in range(NCORE):
            wo_direct(s).wait_recv()
            wo_onward(s).start()

    def wo_arrived():
        @pl.when(wo_here)
        def _():
            wo_stay.wait()
            ref = wog_ref.at[1 - core, k % 2]
            remote(ref, ref, wo_send.at[0], wo_recv.at[1 - core, k % 2], sibling).wait_recv()

        @pl.when(jnp.logical_not(wo_here))
        def _():
            for s in range(NCORE):
                for first in range(2):
                    ref = wog_ref.at[s, k % 2, pl.ds(first * wo_half, wo_half), :]
                    remote(ref, ref, wof_send.at[s], wof_recv.at[s, first], sibling).wait_recv()

    def first_duties():
        for load in loads[1:]:
            load.wait()
        kdim = heads * NOPE
        wkv[:kdim] = wk_ref[...].astype(F32).T.astype(BF16)
        ring_move(1, (0,))
        z_pass(1)
        wkv[kdim:] = wv_ref[...].astype(F32).T.astype(BF16)
        seen = [vis_ref[pl.ds(me, 1), :], vis_ref[pl.ds(2 * NCTX - 1 - me, 1), :]]
        hidden = jnp.concatenate(
            [jnp.broadcast_to(jnp.where(row == 1, 0.0, 1.0), (rows // 2, row.shape[1])) for row in seen], axis=0
        ).astype(BF16)
        for h in range(heads):
            lo = h * (NOPE + ROPE)
            qaug[h] = jnp.concatenate([q_ref[:, lo : lo + NOPE + ROPE], hidden], axis=1)
        i = lax.broadcasted_iota(jnp.int32, diag.shape, 0)
        j = lax.broadcasted_iota(jnp.int32, diag.shape, 1)
        jj = j % rows
        same = (j // rows == k) & (i // (rows // 2) == jj // (rows // 2))
        diag[...] = jnp.where(same & (jj > i), MASKED, 0.0)
        m_ref[...] = jnp.full(m_ref.shape, MASKED, F32)
        acc_ref[...] = jnp.zeros(acc_ref.shape, F32)
        ring_move(2, (0,))
        z_pass(2)
        z_pass(3)
        for copy in wo_far:
            copy.start()

        @pl.when(wo_here)
        def _():
            wo_stay.start()

        @pl.when(jnp.logical_not(wo_here))
        def _():
            wo_pass.start()

        on_core(z_sib_wait)

    def duties(stage):
        if stage <= 4:
            ring_move(stage, range(NZH) if stage == 4 else range(1, NZH))

            @pl.when(core == 0)
            def _():
                for n, yy in groups(stage):
                    low_copy(n, yy).start()

            @pl.when(core == 1)
            def _():
                for n, yy in groups(stage):
                    for q in (1, 2, 3):
                        x_copy(n, yy, q).start()
                    high_copy(n, yy, 0).start()

        if stage == 1:
            ring_move(3, (0,))
        if stage == 4:
            wo_forward()
        if stage == 2:
            diag[...] = jnp.zeros(diag.shape, F32)
        if stage > 1:
            @pl.when(core == 1)
            def _():
                for n, yy in groups(stage - 1):
                    for q in (1, 2, 3):
                        x_wait(n, yy, q)
                        high_copy(n, yy, q).start()
                for n, yy in groups(stage - 1):
                    low_copy(n, yy).wait_recv()

            @pl.when(core == 0)
            def _():
                for n, yy in groups(stage - 1):
                    for q in range(NX):
                        high_copy(n, yy, q).wait_recv()

    factor = math.log2(math.e) / math.sqrt(NOPE + ROPE)
    keys = NZH * rows

    def attend(groups_now, masked):
        firsts = [block_of(yy, 0) for yy in groups_now]
        parts = [all_ref[first + j] for first in firsts for j in range(NZH)]
        count = keys * len(groups_now)
        ids = lax.broadcasted_iota(jnp.int32, (2 * NCTX, keys), 0)
        lane = lax.broadcasted_iota(jnp.int32, (2 * NCTX, keys), 1)
        tails = []
        for i, first in enumerate(firsts):
            source = first + lane // rows
            key_block = jnp.where(lane % rows < rows // 2, source, 2 * NCTX - 1 - source)
            which = jnp.where(ids == key_block, MASKED, 0.0).astype(BF16)
            rotary = jnp.concatenate([p[LATENT:] for p in parts[NZH * i : NZH * (i + 1)]], axis=1)
            tails.append(jnp.concatenate([rotary, which], axis=0))
        kdim = heads * NOPE
        compacts = [
            jnp.concatenate([p[:LATENT] for p in parts[NZH * i : NZH * (i + 1)]], axis=1)
            for i in range(len(firsts))
        ]

        def expand(i, lo, hi):
            kv[lo:hi, i * keys : (i + 1) * keys] = jnp.dot(
                wkv[lo:hi], compacts[i], preferred_element_type=F32
            ).astype(BF16)

        for i in range(len(firsts)):
            expand(i, 0, kdim)
        tail = jnp.concatenate(tails, axis=1)
        ones = jnp.ones((VHEAD, count), BF16)

        def scores(h):
            full = jnp.concatenate([kv[h * NOPE : (h + 1) * NOPE, :count], tail], axis=0)
            s = jnp.dot(qaug[h], full, preferred_element_type=F32)
            return s + diag[...] if masked else s

        def weigh(h, p, alpha):
            row = (heads + h) * VHEAD
            new = nt_dot(p, jnp.concatenate([kv[row : row + VHEAD, :count], ones], axis=0))
            acc_ref[h] = acc_ref[h] * jnp.concatenate([alpha, alpha], axis=1) + new

        following = scores(0)
        waiting = None
        for h in range(heads):
            s = following
            if h + 1 < heads:
                following = scores(h + 1)
            if h < len(firsts):
                expand(h, kdim, 2 * kdim)
            m_old = m_ref[h]
            m_new = jnp.maximum(m_old, jnp.max(s, axis=1, keepdims=True))
            alpha = jnp.exp2((m_old - m_new) * factor)
            p = jnp.exp2((s - m_new[:, :1]) * factor).astype(BF16)
            m_ref[h] = m_new
            if waiting:
                weigh(*waiting)
            waiting = (h, p, alpha)
        weigh(*waiting)

    @pl.loop(0, 6)
    def _(stage):
        @pl.when(stage == 0)
        def _():
            first_duties()

        for v in range(1, 6):
            @pl.when(stage == v)
            def _():
                duties(v)

        @pl.when((stage == 1) | (stage == 5))
        def _():
            attend([y - (stage - 1)], True)

        @pl.when((stage > 1) & (stage < 5))
        def _():
            attend([y - (stage - 1), y + (stage - 1)], False)

    for h in range(heads):
        blocks[core, y, :, h * VHEAD : (h + 1) * VHEAD] = (
            acc_ref[h, :, :VHEAD] / acc_ref[h, :, VHEAD:]
        ).astype(BF16)

    def at(yy):
        return lax.rem(yy + NY, NY)

    def a_copy(going_up, step, t, wait):
        off = step if wait else step - 1
        yy = at(y - off if going_up else y + off)
        ref = blocks.at[core, yy, pl.ds(t * (rows // 2), rows // 2), :]
        send, recv, dev = (ar_send, ar_recv, up) if going_up else (al_send, al_recv, down)
        return remote(ref, ref, send.at[step - 1, t], recv.at[step - 1, t], dev)

    def a_goes(going_up, step, t):
        return step < 4 or (step == 4 and (t == 0) == going_up)

    def a_step(step):
        for t in range(2):
            for going_up in (True, False):
                if a_goes(going_up, step, t):
                    if step > 0:
                        a_copy(going_up, step, t, True).wait_recv()
                    if a_goes(going_up, step + 1, t):
                        a_copy(going_up, step + 1, t, False).start()

    def a_sib(n, yy, here):
        ref = blocks.at[core if here else 1 - core, at(yy)]
        return remote(ref, ref, as_send.at[n], as_recv.at[n], sibling)

    def piece_copy(yy):
        there = (me, lax.rem(y + yy, NCHIP) * NCORE + core)
        return remote(outgoing.at[yy], incoming.at[chip], p_send.at[yy], p_recv.at[chip], there)

    def piece(n, yy):
        a_sib(n, yy, False).wait_recv()
        yy = at(yy)
        acc = nt_dot(wog_ref[0].reshape(out_ref.shape[0], -1), blocks[0, yy])
        acc += nt_dot(wog_ref[1].reshape(out_ref.shape[0], -1), blocks[1, yy])

        @pl.when(yy == mine_y)
        def _():
            kept[...] = acc

        @pl.when(yy != mine_y)
        def _():
            outgoing[yy] = acc.astype(BF16)

        @pl.when(yy != mine_y)
        def _():
            piece_copy(yy).start()

    a_step(0)
    a_sib(0, y, True).start()
    wo_arrived()
    piece(0, y)

    def z_sent(c):
        for j in (1, 2, 3):
            z_copy(c, j).wait_send()
            z_sib(c, j).wait_send()

    on_core(z_sent)
    def ring_sent(row0, count):
        for step in (1, 2, 3, 4):
            for j in range(NZH):
                for going_up in (True, False):
                    if goes(going_up, step, j):
                        ring_copy(going_up, step, j, row0, count, False).wait_send()

    @pl.when(core == 0)
    def _():
        ring_sent(0, low)
        for step in (1, 2, 3, 4):
            for n, yy in groups(step):
                low_copy(n, yy).wait_send()

    @pl.when(core == 1)
    def _():
        ring_sent(mine, quarter)
        for step in (1, 2, 3, 4):
            for n, yy in groups(step):
                for q in (1, 2, 3):
                    x_copy(n, yy, q).wait_send()
                for q in range(NX):
                    high_copy(n, yy, q).wait_send()

    for step in (1, 2, 3):
        a_step(step)
        a_sib(2 * step - 1, y - step, True).start()
        a_sib(2 * step, y + step, True).start()
        piece(2 * step - 1, y - step)
        piece(2 * step, y + step)
    a_step(4)
    a_sib(7, y + 4, True).start()
    piece(7, y + 4)

    total = kept[...]
    for j in range(1, NCHIP):
        source = lax.rem(chip + j, NCHIP)
        ref = incoming.at[source]
        remote(ref, ref, p_send.at[0], p_recv.at[source], chips[j - 1]).wait_recv()
        total += incoming[source].astype(F32)

    @pl.when(jnp.logical_not(moves))
    def _():
        out_ref[...] = total.astype(BF16)

    to_last = remote(final, out_ref, f_send, f_recv, last)

    @pl.when(moves)
    def _():
        final[...] = total.astype(BF16)
        to_last.start()

    for copy in wo_far:
        copy.wait_send()
    for s in range(NCORE):
        wo_onward(s).wait_send()

    @pl.when(jnp.logical_not(wo_here))
    def _():
        wo_pass.wait_send()

    for step in (1, 2, 3, 4):
        for t in range(2):
            for going_up in (True, False):
                if a_goes(going_up, step, t):
                    a_copy(going_up, step, t, False).wait_send()
    for n, off in enumerate((0, -1, 1, -2, 2, -3, 3, 4)):
        a_sib(n, y + off, True).wait_send()
    for j in range(1, NCHIP):
        piece_copy(lax.rem(mine_y + j, NY)).wait_send()

    @pl.when(moves)
    def _():
        to_last.wait()


def on_device(query, latent, w_uk, w_uv, w_o, visible):
    rows, width = latent.shape
    inner, cols = w_o.shape
    heads = w_uk.shape[1] // NOPE
    dma = pltpu.SemaphoreType.DMA
    vmem = pltpu.VMEM
    out = pl.pallas_call(
        layer_kernel,
        out_shape=jax.ShapeDtypeStruct((2 * cols, rows), BF16),
        in_specs=[pl.BlockSpec(memory_space=pl.ANY)] * 6,
        out_specs=pl.BlockSpec(memory_space=pltpu.VMEM),
        scratch_shapes=[
            vmem(query.shape, BF16),
            vmem((width, rows), BF16),
            vmem(w_uk.shape, BF16),
            vmem(w_uv.shape, BF16),
            vmem((cols, inner), BF16),
            vmem(visible.shape, jnp.int32),
            vmem((NCTX, width, rows), BF16),
            vmem((NCORE, 2, cols, inner), BF16),
            vmem((heads * (NOPE + VHEAD), LATENT), BF16),
            vmem((heads * (NOPE + VHEAD), 2 * NZH * rows), BF16),
            vmem((heads, rows, NOPE + ROPE + 2 * NCTX), BF16),
            vmem((rows, NZH * rows), F32),
            vmem((heads, rows, 128), F32),
            vmem((heads, rows, 2 * VHEAD), F32),
            vmem((NCORE, NY, rows, inner), BF16),
            vmem((NCHIP, 2 * cols, rows), BF16),
            vmem((NCHIP, 2 * cols, rows), BF16),
            vmem((2 * cols, rows), F32),
            vmem((2 * cols, rows), BF16),
            dma((6,)),
            dma((3,)),
            dma((3,)),
            dma((4, NZH)),
            dma((4, NZH)),
            dma((4, NZH)),
            dma((4, NZH)),
            dma((7, NX)),
            dma((7, NX)),
            dma((4 + 7 * NX,)),
            dma((4 + 7 * NX,)),
            dma((4,)),
            dma((NCORE, 2)),
            dma((NCORE,)),
            dma((NCORE, 2)),
            dma((4, 2)),
            dma((4, 2)),
            dma((4, 2)),
            dma((4, 2)),
            dma((NY,)),
            dma((NY,)),
            dma((NCHIP,)),
            dma((NCHIP,)),
            dma,
            dma,
        ],
        compiler_params=pltpu.CompilerParams(
            collective_id=0, has_side_effects=True, vmem_limit_bytes=56 << 20
        ),
        name="layer",
    )(query, latent.T, w_uk, w_uv, w_o.T, visible)
    return out.T


def solution(mesh):
    in_specs = (P("ctx", "hg"), P("ctx", None), P(None, "hg"), P(None, "hg"), P("hg", "ctx"), P())
    out_specs = P("ctx", "hg")
    return jax.shard_map(
        on_device, mesh=mesh, in_specs=in_specs, out_specs=out_specs, check_vma=False
    )
```

```python
import math

import jax
import jax.numpy as jnp
from jax import lax
from jax.experimental import pallas as pl
from jax.experimental.pallas import tpu as pltpu
from jax.sharding import PartitionSpec as P

NOPE = 128
ROPE = 64
LATENT = 512
VHEAD = 128
NY, NZH, NZL, NX, NCORE = 8, 4, 2, 4, 2
NCTX = NY * NZH
NCHIP = NZL * NX
MESH = pl.DeviceIdType.MESH
MASKED = -1e30
LOW = 288
BF16 = jnp.bfloat16
F32 = jnp.float32


def place():
    c = lax.axis_index("ctx")
    h = lax.axis_index("hg")
    y, k = c // NZH, c % NZH
    chip, core = h // NCORE, h % NCORE
    zl, x = chip // NX, chip % NX
    return y, k, zl, x, core


def device(y, k, zl, x, core):
    return (
        lax.rem(y + NY, NY) * NZH + lax.rem(k + NZH, NZH),
        (zl * NX + lax.rem(x + NX, NX)) * NCORE + core,
    )


def block_of(y, k):
    return lax.rem(y + NY, NY) * NZH + lax.rem(k + NZH, NZH)


def remote(src, dst, send, recv, dev):
    return pltpu.make_async_remote_copy(
        src_ref=src, dst_ref=dst, send_sem=send, recv_sem=recv, device_id=dev, device_id_type=MESH
    )


def nt_dot(a, b):
    return lax.dot_general(a, b, (((1,), (1,)), ((), ())), preferred_element_type=F32)


def layer_kernel(
    q_hbm,
    lat_hbm,
    wk_hbm,
    wv_hbm,
    wo_hbm,
    vis_hbm,
    out_ref,
    q_ref,
    lat_ref,
    wk_ref,
    wv_ref,
    wo_ref,
    vis_ref,
    all_ref,
    wog_ref,
    wkv,
    kv,
    qaug,
    diag,
    m_ref,
    acc_ref,
    blocks,
    outgoing,
    incoming,
    kept,
    final,
    in_sem,
    z_send,
    z_recv,
    r_send,
    r_recv,
    l_send,
    l_recv,
    x_send,
    x_recv,
    sib_send,
    sib_recv,
    wo_send,
    wo_recv,
    wof_send,
    wof_recv,
    ar_send,
    ar_recv,
    al_send,
    al_recv,
    as_send,
    as_recv,
    p_send,
    p_recv,
    f_send,
    f_recv,
):
    y, k, zl, x, core = place()
    chip = zl * NX + x
    width, rows = lat_ref.shape
    heads = acc_ref.shape[0]
    low = LOW
    high = width - low
    quarter = high // NX
    d = 2 * zl - 1
    me = y * NZH + k
    sibling = device(y, k, zl, x, 1 - core)
    line = [device(y, k + j, zl, x, core) for j in (1, 2, 3)]
    line += [device(y, k + j, zl, x, 1 - core) for j in range(NZH)]
    z_targets = [
        device(y, k + d, 1 - zl, x, core),
        device(y, k + d, zl, x, core),
        device(y, k + 2, 1 - zl, x, core),
    ]
    up, down = device(y + 1, k, zl, x, core), device(y - 1, k, zl, x, core)
    x_peers = [device(y, k, zl, x + j, core) for j in (1, 2, 3)]
    chips = [(me, lax.rem(chip + j, NCHIP) * NCORE + core) for j in range(1, NCHIP)]
    mine_y = lax.rem(chip - y + NY, NY)
    last = (mine_y * NZH + k, y * NCORE + core)
    origin = (chip * NZH + k, lax.rem(y + chip, NCHIP) * NCORE + core)
    moves = (chip != y) | (mine_y != y)

    loads = [
        pltpu.make_async_copy(src, dst, in_sem.at[i])
        for i, (src, dst) in enumerate(
            (
                (lat_hbm, lat_ref),
                (q_hbm, q_ref),
                (vis_hbm, vis_ref),
                (wk_hbm, wk_ref),
                (wv_hbm, wv_ref),
                (wo_hbm, wo_ref),
            )
        )
    ]
    for load in loads:
        load.start()

    partners = line + [z_targets[0], z_targets[2], up, down] + chips
    barrier = pltpu.get_barrier_semaphore()
    for dev in partners:
        pl.semaphore_signal(barrier, inc=1, device_id=dev, device_id_type=MESH)

    @pl.when(moves)
    def _():
        pl.semaphore_signal(barrier, inc=1, device_id=origin, device_id_type=MESH)

    pl.semaphore_wait(barrier, len(partners) + jnp.where(moves, 1, 0))

    loads[0].wait()
    parts_of = (pl.ds(0, low), pl.ds(low, high))
    order = [k, k + d, k - d, k + 2]
    mine = pl.multiple_of(low + x * quarter, 8)

    def on_core(visit):
        for c in range(NCORE):
            @pl.when(core == c)
            def _():
                visit(c)

    def z_copy(c, j):
        src, dst = lat_ref.at[parts_of[c], :], all_ref.at[me, parts_of[c], :]
        return remote(src, dst, z_send.at[j - 1], z_recv.at[j - 1], z_targets[j - 1])

    def z_start(c):
        for j in (1, 2, 3):
            z_copy(c, j).start()

    on_core(z_start)
    all_ref[me] = lat_ref[...]

    def z_sib(c, j):
        ref = all_ref.at[block_of(y, order[j]), parts_of[c], :]
        return remote(ref, ref, sib_send.at[j], sib_recv.at[j], sibling)

    def z_pass(j):
        def visit(c):
            ref = all_ref.at[block_of(y, order[j]), parts_of[c], :]
            remote(ref, ref, z_send.at[j - 1], z_recv.at[j - 1], z_targets[j - 1]).wait_recv()
            z_sib(c, j).start()

        on_core(visit)
        ring_start(j)

    def z_sib_wait(c):
        for j in (1, 2, 3):
            z_sib(1 - c, j).wait_recv()

    def ring_copy(going_up, step, j, row0, count, wait):
        off = step if wait else step - 1
        yy = y - off if going_up else y + off
        ref = all_ref.at[block_of(yy, order[j]), pl.ds(row0, count), :]
        send, recv, dev = (r_send, r_recv, up) if going_up else (l_send, l_recv, down)
        return remote(ref, ref, send.at[step - 1, j], recv.at[step - 1, j], dev)

    def goes(going_up, step, j):
        return step < 4 or (step == 4 and (j < 2) == going_up)

    def ring_move(step, blocks_moved):
        def visit(c):
            span = ((0, low), (mine, quarter))[c]
            for j in blocks_moved:
                for going_up in (True, False):
                    if goes(going_up, step, j):
                        ring_copy(going_up, step, j, *span, True).wait_recv()
                        if goes(going_up, step + 1, j):
                            ring_copy(going_up, step + 1, j, *span, False).start()

        on_core(visit)

    def groups(step):
        if step == 4:
            return [(6, y - 4)]
        return [(2 * step - 2, y - step), (2 * step - 1, y + step)]

    def group(yy, row0, count):
        return all_ref.at[pl.ds(block_of(yy, 0), NZH), pl.ds(row0, count), :]

    def low_copy(n, yy):
        ref = group(yy, 0, low)
        return remote(ref, ref, sib_send.at[4 + n * NX], sib_recv.at[4 + n * NX], sibling)

    def high_copy(n, yy, q):
        ref = group(yy, pl.multiple_of(low + lax.rem(x + q, NX) * quarter, 8), quarter)
        slot = 4 + n * NX + q
        return remote(ref, ref, sib_send.at[slot], sib_recv.at[slot], sibling)

    def x_copy(n, yy, q):
        ref = group(yy, mine, quarter)
        return remote(ref, ref, x_send.at[n, q], x_recv.at[n, q], x_peers[q - 1])

    def x_wait(n, yy, q):
        ref = group(yy, pl.multiple_of(low + lax.rem(x + q, NX) * quarter, 8), quarter)
        remote(ref, ref, x_send.at[n, NX - q], x_recv.at[n, NX - q], x_peers[q - 1]).wait_recv()

    def ring_start(j):
        @pl.when(core == 0)
        def _():
            ring_copy(True, 1, j, 0, low, False).start()
            ring_copy(False, 1, j, 0, low, False).start()

        @pl.when(core == 1)
        def _():
            ring_copy(True, 1, j, mine, quarter, False).start()
            ring_copy(False, 1, j, mine, quarter, False).start()

    ring_start(0)

    wo_slot = wog_ref.at[core, k % 2]
    wo_here = core == k // 2
    wo_stay = pltpu.make_async_copy(wo_ref, wo_slot, wo_send.at[0])
    wo_pass = remote(wo_ref, wo_slot, wo_send.at[0], wo_recv.at[core, k % 2], sibling)
    wo_far = [
        remote(wo_ref, wo_slot, wo_send.at[j], wo_recv.at[core, k % 2], device(y, k + j, zl, x, k // 2))
        for j in (1, 3)
    ]
    side = jnp.where(lax.rem(k + 1, NZH) // 2 == core, 1, -1)
    wo_half = wo_ref.shape[0] // 2

    def wo_direct(s):
        ref = wog_ref.at[s, (k + 1) % 2]
        return remote(ref, ref, wo_send.at[0], wo_recv.at[s, (k + 1) % 2], sibling)

    def wo_onward(s):
        first = (1 + side) // 2
        ref = wog_ref.at[s, (k + 1) % 2, pl.ds(pl.multiple_of(first * wo_half, 8), wo_half), :]
        return remote(ref, ref, wof_send.at[s], wof_recv.at[s, first], device(y, k - side, zl, x, core))

    def wo_forward():
        for s in range(NCORE):
            wo_direct(s).wait_recv()
            wo_onward(s).start()

    def wo_arrived():
        @pl.when(wo_here)
        def _():
            wo_stay.wait()
            ref = wog_ref.at[1 - core, k % 2]
            remote(ref, ref, wo_send.at[0], wo_recv.at[1 - core, k % 2], sibling).wait_recv()

        @pl.when(jnp.logical_not(wo_here))
        def _():
            for s in range(NCORE):
                for first in range(2):
                    ref = wog_ref.at[s, k % 2, pl.ds(first * wo_half, wo_half), :]
                    remote(ref, ref, wof_send.at[s], wof_recv.at[s, first], sibling).wait_recv()

    def first_duties():
        for load in loads[1:]:
            load.wait()
        kdim = heads * NOPE
        wkv[:kdim] = wk_ref[...].astype(F32).T.astype(BF16)
        ring_move(1, (0,))
        z_pass(1)
        wkv[kdim:] = wv_ref[...].astype(F32).T.astype(BF16)
        seen = [vis_ref[pl.ds(me, 1), :], vis_ref[pl.ds(2 * NCTX - 1 - me, 1), :]]
        hidden = jnp.concatenate(
            [jnp.broadcast_to(jnp.where(row == 1, 0.0, 1.0), (rows // 2, row.shape[1])) for row in seen], axis=0
        ).astype(BF16)
        for h in range(heads):
            lo = h * (NOPE + ROPE)
            qaug[h] = jnp.concatenate([q_ref[:, lo : lo + NOPE + ROPE], hidden], axis=1)
        i = lax.broadcasted_iota(jnp.int32, diag.shape, 0)
        j = lax.broadcasted_iota(jnp.int32, diag.shape, 1)
        jj = j % rows
        same = (j // rows == k) & (i // (rows // 2) == jj // (rows // 2))
        diag[...] = jnp.where(same & (jj > i), MASKED, 0.0)
        m_ref[...] = jnp.full(m_ref.shape, MASKED, F32)
        acc_ref[...] = jnp.zeros(acc_ref.shape, F32)
        ring_move(2, (0,))
        z_pass(2)
        z_pass(3)
        for copy in wo_far:
            copy.start()

        @pl.when(wo_here)
        def _():
            wo_stay.start()

        @pl.when(jnp.logical_not(wo_here))
        def _():
            wo_pass.start()

        on_core(z_sib_wait)

    def duties(stage):
        if stage <= 4:
            ring_move(stage, range(NZH) if stage == 4 else range(1, NZH))

            @pl.when(core == 0)
            def _():
                for n, yy in groups(stage):
                    low_copy(n, yy).start()

            @pl.when(core == 1)
            def _():
                for n, yy in groups(stage):
                    for q in (1, 2, 3):
                        x_copy(n, yy, q).start()
                    high_copy(n, yy, 0).start()

        if stage == 1:
            ring_move(3, (0,))
        if stage == 4:
            wo_forward()
        if stage == 2:
            diag[...] = jnp.zeros(diag.shape, F32)
        if stage > 1:
            @pl.when(core == 1)
            def _():
                for n, yy in groups(stage - 1):
                    for q in (1, 2, 3):
                        x_wait(n, yy, q)
                        high_copy(n, yy, q).start()
                for n, yy in groups(stage - 1):
                    low_copy(n, yy).wait_recv()

            @pl.when(core == 0)
            def _():
                for n, yy in groups(stage - 1):
                    for q in range(NX):
                        high_copy(n, yy, q).wait_recv()

    factor = math.log2(math.e) / math.sqrt(NOPE + ROPE)
    keys = NZH * rows

    def attend(groups_now, masked):
        firsts = [block_of(yy, 0) for yy in groups_now]
        parts = [all_ref[first + j] for first in firsts for j in range(NZH)]
        count = keys * len(groups_now)
        ids = lax.broadcasted_iota(jnp.int32, (2 * NCTX, keys), 0)
        lane = lax.broadcasted_iota(jnp.int32, (2 * NCTX, keys), 1)
        tails = []
        for i, first in enumerate(firsts):
            source = first + lane // rows
            key_block = jnp.where(lane % rows < rows // 2, source, 2 * NCTX - 1 - source)
            which = jnp.where(ids == key_block, MASKED, 0.0).astype(BF16)
            rotary = jnp.concatenate([p[LATENT:] for p in parts[NZH * i : NZH * (i + 1)]], axis=1)
            tails.append(jnp.concatenate([rotary, which], axis=0))
        kdim = heads * NOPE
        compacts = [
            jnp.concatenate([p[:LATENT] for p in parts[NZH * i : NZH * (i + 1)]], axis=1)
            for i in range(len(firsts))
        ]

        def expand(i, lo, hi):
            kv[lo:hi, i * keys : (i + 1) * keys] = jnp.dot(
                wkv[lo:hi], compacts[i], preferred_element_type=F32
            ).astype(BF16)

        for i in range(len(firsts)):
            expand(i, 0, kdim)
        tail = jnp.concatenate(tails, axis=1)
        ones = jnp.ones((VHEAD, count), BF16)

        def scores(h):
            full = jnp.concatenate([kv[h * NOPE : (h + 1) * NOPE, :count], tail], axis=0)
            s = jnp.dot(qaug[h], full, preferred_element_type=F32)
            return s + diag[...] if masked else s

        def weigh(h, p, alpha):
            row = (heads + h) * VHEAD
            new = nt_dot(p, jnp.concatenate([kv[row : row + VHEAD, :count], ones], axis=0))
            acc_ref[h] = acc_ref[h] * jnp.concatenate([alpha, alpha], axis=1) + new

        following = scores(0)
        waiting = None
        for h in range(heads):
            s = following
            if h + 1 < heads:
                following = scores(h + 1)
            if h < len(firsts):
                expand(h, kdim, 2 * kdim)
            m_old = m_ref[h]
            m_new = jnp.maximum(m_old, jnp.max(s, axis=1, keepdims=True))
            alpha = jnp.exp2((m_old - m_new) * factor)
            p = jnp.exp2((s - m_new[:, :1]) * factor).astype(BF16)
            m_ref[h] = m_new
            if waiting:
                weigh(*waiting)
            waiting = (h, p, alpha)
        weigh(*waiting)

    @pl.loop(0, 6)
    def _(stage):
        @pl.when(stage == 0)
        def _():
            first_duties()

        for v in range(1, 6):
            @pl.when(stage == v)
            def _():
                duties(v)

        @pl.when((stage == 1) | (stage == 5))
        def _():
            attend([y - (stage - 1)], True)

        @pl.when((stage > 1) & (stage < 5))
        def _():
            attend([y - (stage - 1), y + (stage - 1)], False)

    for h in range(heads):
        blocks[core, y, :, h * VHEAD : (h + 1) * VHEAD] = (
            acc_ref[h, :, :VHEAD] / acc_ref[h, :, VHEAD:]
        ).astype(BF16)

    def at(yy):
        return lax.rem(yy + NY, NY)

    def a_copy(going_up, step, t, wait):
        off = step if wait else step - 1
        yy = at(y - off if going_up else y + off)
        ref = blocks.at[core, yy, pl.ds(t * (rows // 2), rows // 2), :]
        send, recv, dev = (ar_send, ar_recv, up) if going_up else (al_send, al_recv, down)
        return remote(ref, ref, send.at[step - 1, t], recv.at[step - 1, t], dev)

    def a_goes(going_up, step, t):
        return step < 4 or (step == 4 and (t == 0) == going_up)

    def a_step(step):
        for t in range(2):
            for going_up in (True, False):
                if a_goes(going_up, step, t):
                    if step > 0:
                        a_copy(going_up, step, t, True).wait_recv()
                    if a_goes(going_up, step + 1, t):
                        a_copy(going_up, step + 1, t, False).start()

    def a_sib(n, yy, here):
        ref = blocks.at[core if here else 1 - core, at(yy)]
        return remote(ref, ref, as_send.at[n], as_recv.at[n], sibling)

    def piece_copy(yy):
        there = (me, lax.rem(y + yy, NCHIP) * NCORE + core)
        return remote(outgoing.at[yy], incoming.at[chip], p_send.at[yy], p_recv.at[chip], there)

    def piece(n, yy):
        a_sib(n, yy, False).wait_recv()
        yy = at(yy)
        acc = nt_dot(wog_ref[0].reshape(out_ref.shape[0], -1), blocks[0, yy])
        acc += nt_dot(wog_ref[1].reshape(out_ref.shape[0], -1), blocks[1, yy])

        @pl.when(yy == mine_y)
        def _():
            kept[...] = acc

        @pl.when(yy != mine_y)
        def _():
            outgoing[yy] = acc.astype(BF16)

        @pl.when(yy != mine_y)
        def _():
            piece_copy(yy).start()

    a_step(0)
    a_sib(0, y, True).start()
    wo_arrived()
    piece(0, y)

    def z_sent(c):
        for j in (1, 2, 3):
            z_copy(c, j).wait_send()
            z_sib(c, j).wait_send()

    on_core(z_sent)
    def ring_sent(row0, count):
        for step in (1, 2, 3, 4):
            for j in range(NZH):
                for going_up in (True, False):
                    if goes(going_up, step, j):
                        ring_copy(going_up, step, j, row0, count, False).wait_send()

    @pl.when(core == 0)
    def _():
        ring_sent(0, low)
        for step in (1, 2, 3, 4):
            for n, yy in groups(step):
                low_copy(n, yy).wait_send()

    @pl.when(core == 1)
    def _():
        ring_sent(mine, quarter)
        for step in (1, 2, 3, 4):
            for n, yy in groups(step):
                for q in (1, 2, 3):
                    x_copy(n, yy, q).wait_send()
                for q in range(NX):
                    high_copy(n, yy, q).wait_send()

    for step in (1, 2, 3):
        a_step(step)
        a_sib(2 * step - 1, y - step, True).start()
        a_sib(2 * step, y + step, True).start()
        piece(2 * step - 1, y - step)
        piece(2 * step, y + step)
    a_step(4)
    a_sib(7, y + 4, True).start()
    piece(7, y + 4)

    total = kept[...]
    for j in range(1, NCHIP):
        source = lax.rem(chip + j, NCHIP)
        ref = incoming.at[source]
        remote(ref, ref, p_send.at[0], p_recv.at[source], chips[j - 1]).wait_recv()
        total += incoming[source].astype(F32)

    @pl.when(jnp.logical_not(moves))
    def _():
        out_ref[...] = total.astype(BF16)

    to_last = remote(final, out_ref, f_send, f_recv, last)

    @pl.when(moves)
    def _():
        final[...] = total.astype(BF16)
        to_last.start()

    for copy in wo_far:
        copy.wait_send()
    for s in range(NCORE):
        wo_onward(s).wait_send()

    @pl.when(jnp.logical_not(wo_here))
    def _():
        wo_pass.wait_send()

    for step in (1, 2, 3, 4):
        for t in range(2):
            for going_up in (True, False):
                if a_goes(going_up, step, t):
                    a_copy(going_up, step, t, False).wait_send()
    for n, off in enumerate((0, -1, 1, -2, 2, -3, 3, 4)):
        a_sib(n, y + off, True).wait_send()
    for j in range(1, NCHIP):
        piece_copy(lax.rem(mine_y + j, NY)).wait_send()

    @pl.when(moves)
    def _():
        to_last.wait()


def on_device(query, latent, w_uk, w_uv, w_o, visible):
    rows, width = latent.shape
    inner, cols = w_o.shape
    heads = w_uk.shape[1] // NOPE
    dma = pltpu.SemaphoreType.DMA
    vmem = pltpu.VMEM
    out = pl.pallas_call(
        layer_kernel,
        out_shape=jax.ShapeDtypeStruct((2 * cols, rows), BF16),
        in_specs=[pl.BlockSpec(memory_space=pl.ANY)] * 6,
        out_specs=pl.BlockSpec(memory_space=pltpu.VMEM),
        scratch_shapes=[
            vmem(query.shape, BF16),
            vmem((width, rows), BF16),
            vmem(w_uk.shape, BF16),
            vmem(w_uv.shape, BF16),
            vmem((cols, inner), BF16),
            vmem(visible.shape, jnp.int32),
            vmem((NCTX, width, rows), BF16),
            vmem((NCORE, 2, cols, inner), BF16),
            vmem((heads * (NOPE + VHEAD), LATENT), BF16),
            vmem((heads * (NOPE + VHEAD), 2 * NZH * rows), BF16),
            vmem((heads, rows, NOPE + ROPE + 2 * NCTX), BF16),
            vmem((rows, NZH * rows), F32),
            vmem((heads, rows, 128), F32),
            vmem((heads, rows, 2 * VHEAD), F32),
            vmem((NCORE, NY, rows, inner), BF16),
            vmem((NCHIP, 2 * cols, rows), BF16),
            vmem((NCHIP, 2 * cols, rows), BF16),
            vmem((2 * cols, rows), F32),
            vmem((2 * cols, rows), BF16),
            dma((6,)),
            dma((3,)),
            dma((3,)),
            dma((4, NZH)),
            dma((4, NZH)),
            dma((4, NZH)),
            dma((4, NZH)),
            dma((7, NX)),
            dma((7, NX)),
            dma((4 + 7 * NX,)),
            dma((4 + 7 * NX,)),
            dma((4,)),
            dma((NCORE, 2)),
            dma((NCORE,)),
            dma((NCORE, 2)),
            dma((4, 2)),
            dma((4, 2)),
            dma((4, 2)),
            dma((4, 2)),
            dma((NY,)),
            dma((NY,)),
            dma((NCHIP,)),
            dma((NCHIP,)),
            dma,
            dma,
        ],
        compiler_params=pltpu.CompilerParams(
            collective_id=0, has_side_effects=True, vmem_limit_bytes=56 << 20
        ),
        name="layer",
    )(query, latent.T, w_uk, w_uv, w_o.T, visible)
    return out.T


def solution(mesh):
    in_specs = (P("ctx", "hg"), P("ctx", None), P(None, "hg"), P(None, "hg"), P("hg", "ctx"), P())
    out_specs = P("ctx", "hg")
    return jax.shard_map(
        on_device, mesh=mesh, in_specs=in_specs, out_specs=out_specs, check_vma=False
    )
```
